256 devices in a mesh: group: 16 (over z_lo, y), tok: 16 (over z_hi, x, core).
Axes of the slice: x: 4, y: 4, z: 8 (z_hi: 2, z_lo: 4; z = z_hi * 4 + z_lo), core: 2. Of those that a mesh axis runs over, the one named last changes fastest.
Arguments:
- tokens: bfloat16 [131072, 2048], P(('group', 'tok')), may hold values from -94 to 94
- learning_rates: float32 [2, 131072], P(None, 'group'), may hold values from 0.1 to 1
- channel_gains: float32 [2, 5, 2048], P(None, None, 'tok'), may hold values from 0.3 to 3
- fast_init: float32 [2, 3, 16, 128, 128], P(None, None, 'tok'), may hold values from -0.5 to 0.5
- step_size: float32 [2, 16], P(None, 'tok'), may hold values from 0.05 to 1
- update_table: int32 [2, 16], replicated, may hold values 0 or 1
Outputs:
- mixed: bfloat16 [131072, 2048], P(('group', 'tok'))
The draws below stay inside these ranges and needn't reach their ends.
All inputs are finite; a program needn't handle non-finite values.
Results may differ from the reference program's by a relative error of at most 0.033.
Values may be sent and summed in bfloat16 or wider, within the bound.
No kernel may reach another device: no remote copies, remote signals or barrier semaphores. Data moves between devices by JAX's collectives and lax.ppermute only.
A program may use at most 64 MiB of HBM per device.

```python
import math
import jax
import jax.numpy as jnp
from jax import lax

D = 2048
HEADS = 16
HEAD = 128
LAYERS = 2
NS_STEPS = 5
GROUPS = 16
GROUP_TOK = 8192
TOKENS = 131072


def draw_tokens(key, part):
    key_base = jax.random.fold_in(key, 11)
    key_jitter = jax.random.fold_in(key, 12)
    normal_draw = jnp.clip(jax.random.normal(key_base, (TOKENS, D), jnp.float32), -6.0, 6.0)
    channel_ramp = 3.0 ** (jnp.arange(D, dtype=jnp.float32) / D)
    jitter = jax.random.uniform(key_jitter, (D,), jnp.float32, 0.7, 1.3)
    values = normal_draw * (channel_ramp * jitter)[None, :]
    return values.astype(jnp.bfloat16)


def plant(array, own_key, least, largest):
    extent = array.shape
    index_at = [jax.random.randint(jax.random.fold_in(own_key, axis), (), 0, extent[axis]) for axis in range(len(extent))]
    array = array.at[tuple(index_at)].set(least)
    longest = extent.index(max(extent))
    index_at[longest] = (index_at[longest] + 1) % extent[longest]
    return array.at[tuple(index_at)].set(largest)


def steps_of(rng, dims, cuts, least, largest):
    def one(dim, shards_of):
        heights = jax.random.uniform(jax.random.fold_in(jax.random.fold_in(rng, 6), dim), (shards_of,), jnp.float32, least / len(cuts), largest / len(cuts))
        return jnp.repeat(jnp.exp(heights), dims[dim] // shards_of).reshape((-1,) + (1,) * (len(dims) - dim - 1))

    loudness = one(*cuts[0])
    for cut in cuts[1:]:
        loudness = loudness * one(*cut)
    return loudness


def normal_values(own_key, shape, deviation, most, pieces=(), held_as=jnp.bfloat16):
    level = steps_of(own_key, shape, pieces, -0.22, 0.18) if pieces else 1.0
    result = jax.random.normal(own_key, shape, jnp.float32) * deviation * level
    return jnp.minimum(jnp.maximum(result, -most), most).astype(held_as)


def setup_inputs(seed: int = 0) -> dict:
    splits = jax.random.split(jax.random.key(seed), 7)
    return {
        "tokens": draw_tokens(jax.random.fold_in(splits[6], 71), 0),
        "learning_rates": jnp.clip(jnp.exp(math.log(1.0) - 2.3025851 * jax.random.uniform(splits[1], (LAYERS, TOKENS), jnp.float32) ** steps_of(splits[1], (LAYERS, TOKENS), ((1, 16),), -0.2, 0.2)), 0.1, 1.0),
        "channel_gains": jnp.clip(jnp.exp(math.log(3.0) - 2.3025851 * jax.random.uniform(splits[2], (LAYERS, 5, D), jnp.float32) ** steps_of(splits[2], (LAYERS, 5, D), ((2, 16),), -0.2, 0.2)), 0.3, 3.0),
        "fast_init": normal_values(splits[3], (LAYERS, 3, HEADS, HEAD, HEAD), HEAD ** -0.5, 0.5, ((2, 16),), jnp.float32),
        "step_size": jnp.clip(jnp.exp(math.log(1.0) - 2.9957323 * jax.random.uniform(splits[4], (LAYERS, HEADS), jnp.float32) ** steps_of(splits[4], (LAYERS, HEADS), ((1, 16),), -0.2, 0.2)), 0.05, 1.0),
        "update_table": plant((jax.random.randint(splits[5], (LAYERS, GROUPS), 0, 4) < 3).astype(jnp.int32), jax.random.fold_in(splits[5], 1), 0, 1),
    }


MUON_A = 3.4445
MUON_B = -4.775
MUON_C = 2.0315
EPSILON = 1e-06

def orthogonalize(gradient):
    scaling = lax.rsqrt(lax.optimization_barrier(jnp.sum(gradient * gradient, axis=(-2, -1), keepdims=True)) + EPSILON)
    current = gradient * scaling
    for repeat in range(NS_STEPS):
        square = jnp.einsum('...ij,...kj->...ik', current, current, precision=lax.Precision.HIGHEST)
        polynom = MUON_B * square + MUON_C * jnp.einsum('...ij,...jk->...ik', square, square, precision=lax.Precision.HIGHEST)
        current = MUON_A * current + jnp.einsum('...ij,...jk->...ik', polynom, current, precision=lax.Precision.HIGHEST)
    return current

def layer_group(stream, entering, gain_rows, rates_row, steps_row, update_flag, inverse):
    row_count, channel_count = stream.shape
    heads_n = entering.shape[1]
    head_dim = entering.shape[2]
    normed = stream.astype(jnp.float32) * inverse[:, None] * gain_rows[0]
    queries = (normed * gain_rows[1]).astype(jnp.bfloat16).reshape(row_count, heads_n, head_dim).astype(jnp.float32)
    keys_in = (normed * gain_rows[2]).astype(jnp.bfloat16).reshape(row_count, heads_n, head_dim).astype(jnp.float32)
    values_in = (normed * gain_rows[3]).astype(jnp.bfloat16).reshape(row_count, heads_n, head_dim).astype(jnp.float32)
    rounded = entering.astype(jnp.bfloat16).astype(jnp.float32)
    gate_q = jnp.einsum('thi,hij->thj', queries, rounded[0])
    up_q = jnp.einsum('thi,hij->thj', queries, rounded[1])
    hidden_q = (jax.nn.silu(gate_q) * up_q).astype(jnp.bfloat16).astype(jnp.float32)
    output = jnp.einsum('thj,hjk->thk', hidden_q, rounded[2]).reshape(row_count, channel_count)
    mixed_rows = (stream.astype(jnp.float32) + gain_rows[4] * output).astype(jnp.bfloat16)
    gate_k = jnp.einsum('thi,hij->thj', keys_in, rounded[0])
    up_k = jnp.einsum('thi,hij->thj', keys_in, rounded[1])
    sigmoid_k = jax.nn.sigmoid(gate_k)
    active_k = gate_k * sigmoid_k
    hidden_k = (active_k * up_k).astype(jnp.bfloat16).astype(jnp.float32)
    targets = (rates_row[:, None, None] * values_in).astype(jnp.bfloat16).astype(jnp.float32)
    back_hidden = jnp.einsum('thk,hjk->thj', targets, rounded[2])
    back_up = (back_hidden * active_k).astype(jnp.bfloat16).astype(jnp.float32)
    back_gate = (back_hidden * up_k * sigmoid_k * (1.0 + gate_k * (1.0 - sigmoid_k))).astype(jnp.bfloat16).astype(jnp.float32)
    grad_gate = jnp.einsum('thi,thj->hij', keys_in, back_gate)
    grad_up = jnp.einsum('thi,thj->hij', keys_in, back_up)
    grad_down = jnp.einsum('thj,thk->hjk', hidden_k, targets)
    direction = orthogonalize(jnp.stack([grad_gate, grad_up, grad_down]))
    moved_state = entering + (update_flag * steps_row)[None, :, None, None] * direction
    norm_before = jnp.sqrt(lax.optimization_barrier(jnp.sum(entering * entering, axis=2, keepdims=True)) + EPSILON)
    norm_after = jnp.sqrt(lax.optimization_barrier(jnp.sum(moved_state * moved_state, axis=2, keepdims=True)) + EPSILON)
    return (mixed_rows, moved_state * (norm_before / norm_after))

def reference(tokens, learning_rates, channel_gains, fast_init, step_size, update_table):
    stream = tokens.reshape(GROUPS, GROUP_TOK, D)
    for layer_index in range(LAYERS):

        def advance(weights, inputs):
            block_rows, rates_row, update_flag = inputs
            widened = block_rows.astype(jnp.float32)
            inverse = lax.rsqrt(lax.optimization_barrier(jnp.sum(widened * widened, axis=1)) / D + EPSILON)
            mixed_rows, updated = layer_group(block_rows, weights, channel_gains[layer_index], rates_row, step_size[layer_index], update_flag, inverse)
            return (updated, mixed_rows)
        rates_blocks = learning_rates[layer_index].reshape(GROUPS, GROUP_TOK)
        flags = update_table[layer_index].astype(jnp.float32)
        last_state, stream = lax.scan(advance, fast_init[layer_index], (stream, rates_blocks, flags))
    return stream.reshape(TOKENS, D)
```

```python
import functools

import jax
import jax.numpy as jnp
from jax import lax
from jax.experimental import pallas as pl
from jax.experimental.pallas import tpu as pltpu
from jax.sharding import PartitionSpec as P

NS_STEPS = 5
MUON_A = 3.4445
MUON_B = -4.775
MUON_C = 2.0315
EPSILON = 1e-06
CODES = 32767.0
LANES = 128
VMEM_LIMIT = 40 * 1024 * 1024

bf16 = jnp.bfloat16
f32 = jnp.float32


def on_chip():
    return pl.BlockSpec(memory_space=pltpu.VMEM)


def params():
    return pltpu.CompilerParams(vmem_limit_bytes=VMEM_LIMIT)


def dot(left, right):
    return jnp.dot(left, right, preferred_element_type=f32)


def two_parts(value):
    high = value.astype(bf16)
    return high, (value - high.astype(f32)).astype(bf16)


def dot_parts(left, right):
    (lh, ll), (rh, rl) = left, right
    width = rh.shape[1]
    weights = jnp.concatenate(
        [jnp.concatenate([rh, rl], axis=1), jnp.concatenate([rh, jnp.zeros_like(rl)], axis=1)], axis=0
    )
    both = dot(jnp.concatenate([lh, ll], axis=1), weights)
    return both[:, :width] + both[:, width:]


def orthogonalize(gradients):
    current = [
        g * lax.rsqrt(jnp.sum(jnp.sum(g * g, axis=1, keepdims=True), axis=0, keepdims=True) + EPSILON)
        for g in gradients
    ]
    for _ in range(NS_STEPS):
        parts = [two_parts(x) for x in current]
        turned = [two_parts(x.T) for x in current]
        square = [dot_parts(p, t) for p, t in zip(parts, turned)]
        halves = [two_parts(s) for s in square]
        polynom = [MUON_B * s + MUON_C * dot_parts(h, h) for s, h in zip(square, halves)]
        current = [
            MUON_A * x + dot_parts(two_parts(q), p) for x, q, p in zip(current, polynom, parts)
        ]
    return current


def moved_on(weights, step, direction, axis):
    moved = weights + step * direction
    before = jnp.sqrt(jnp.sum(weights * weights, axis=axis, keepdims=True) + EPSILON)
    after = jnp.sqrt(jnp.sum(moved * moved, axis=axis, keepdims=True) + EPSILON)
    return moved * (before / after)


def encode(weights, inverse_unit):
    codes = jnp.clip(jnp.round(weights * inverse_unit), -CODES, CODES)
    return codes.astype(jnp.int32).astype(jnp.int16)


def decode(codes, unit):
    return codes.astype(jnp.int32).astype(f32) * unit


def setup_body(slack, init_ref, code_ref, unit_ref, inverse_ref):
    for index in range(init_ref.shape[0]):
        weights = init_ref[index]
        down = index % 3 == 2
        if down:
            weights = weights.T
        total = jnp.sum(weights * weights, axis=1 if down else 0, keepdims=True) + slack
        unit = jnp.broadcast_to(jnp.sqrt(total) * (1.001 / CODES), weights.shape)
        inverse = 1.0 / unit
        unit_ref[index] = unit
        inverse_ref[index] = inverse
        code_ref[index] = encode(weights, inverse)


def setup(fast_init, groups):
    flat = fast_init.reshape((-1,) + fast_init.shape[-2:])
    return pl.pallas_call(
        functools.partial(setup_body, (groups + 2) * EPSILON),
        out_shape=(
            jax.ShapeDtypeStruct(flat.shape, jnp.int16),
            jax.ShapeDtypeStruct(flat.shape, f32),
            jax.ShapeDtypeStruct(flat.shape, f32),
        ),
        in_specs=[on_chip()],
        out_specs=(on_chip(),) * 3,
        compiler_params=params(),
        name="setup",
    )(flat)


def pack_body(x_ref, o_ref):
    rows, width = x_ref.shape
    heads = width // LANES
    total = jnp.zeros((rows, LANES), f32)
    for head in range(heads):
        piece = x_ref[:, head * LANES : (head + 1) * LANES]
        o_ref[head, :rows, :] = piece
        wide = piece.astype(f32)
        total = total + wide * wide
    lines = [
        jnp.sum(total[r * LANES : (r + 1) * LANES].T, axis=0, keepdims=True) for r in range(rows // LANES)
    ]
    inverse = lax.rsqrt(jnp.concatenate(lines, axis=0) / width + EPSILON)
    high = inverse.astype(bf16).astype(f32)
    middle = (inverse - high).astype(bf16).astype(f32)
    low = inverse - high - middle
    tail = jnp.concatenate([high, middle, low, jnp.zeros_like(low)], axis=0).astype(bf16)
    for head in range(heads):
        o_ref[head, rows:, :] = tail


def pack(x):
    rows, width = x.shape
    tail = 4 * (rows // LANES)
    return pl.pallas_call(
        pack_body,
        out_shape=jax.ShapeDtypeStruct((width // LANES, rows + tail, LANES), bf16),
        compiler_params=params(),
        name="pack",
    )(x)


def prep_body(inverse_inside, rows, *refs):
    if inverse_inside:
        x_ref, rate_ref, gain_ref, k_ref, kt_ref, t_ref, tt_ref, inverse_out = refs
    else:
        x_ref, inverse_ref, rate_ref, gain_ref, k_ref, kt_ref, t_ref, tt_ref = refs
    lines = rows // LANES
    norm = jnp.broadcast_to(gain_ref[:, 0:1], (LANES, LANES))
    key = jnp.broadcast_to(gain_ref[:, 2:3], (LANES, LANES))
    value = jnp.broadcast_to(gain_ref[:, 3:4], (LANES, LANES))

    def one(block, carry):
        if inverse_inside:
            tail = x_ref[block, rows:, :].astype(f32)
            inverse = tail[:lines] + tail[lines : 2 * lines] + tail[2 * lines : 3 * lines]
            inverse_out[block] = inverse
        else:
            inverse = inverse_ref[block]
        rate = rate_ref[block]
        for r in range(lines):
            at = pl.multiple_of(block * rows + r * LANES, LANES)
            turned = x_ref[block, r * LANES : (r + 1) * LANES, :].T.astype(f32)
            normed = turned * inverse[r : r + 1] * norm
            keys = (normed * key).astype(bf16)
            values = (normed * value).astype(bf16)
            targets = (rate[r : r + 1] * values.astype(f32)).astype(bf16)
            kt_ref[:, pl.ds(at, LANES)] = keys
            tt_ref[:, pl.ds(at, LANES)] = targets
            k_ref[pl.ds(at, LANES), :] = keys.T
            t_ref[pl.ds(at, LANES), :] = targets.T
        return carry

    lax.fori_loop(0, x_ref.shape[0], one, 0)


def prep(x, inverse, rates, gains, rows):
    blocks = x.shape[0]
    tall = jax.ShapeDtypeStruct((blocks * rows, LANES), bf16)
    flat = jax.ShapeDtypeStruct((LANES, blocks * rows), bf16)
    inside = inverse is None
    shapes = [tall, flat, tall, flat]
    operands = [x, rates, gains] if inside else [x, inverse, rates, gains]
    if inside:
        shapes.append(jax.ShapeDtypeStruct((blocks, rows // LANES, LANES), f32))
    return pl.pallas_call(
        functools.partial(prep_body, inside, rows),
        out_shape=tuple(shapes),
        in_specs=[on_chip()] * len(operands),
        out_specs=(on_chip(),) * len(shapes),
        compiler_params=params(),
        name="prep",
    )(*operands)


def tick_body(chunk, step_ref, w_ref, unit_ref, inverse_ref, k_ref, kt_ref, t_ref, tt_ref, o_ref):
    weights = [decode(w_ref[j], unit_ref[j]) for j in range(3)]
    gate_up = jnp.concatenate([weights[0].astype(bf16), weights[1].astype(bf16)], axis=1)
    down = weights[2].astype(bf16)

    def part(at):
        both = dot(k_ref[at : at + chunk, :], gate_up)
        back = dot(t_ref[at : at + chunk, :], down)
        gate, up = both[:, :LANES], both[:, LANES:]
        sig = 0.5 * jnp.tanh(0.5 * gate) + 0.5
        act = gate * sig
        hidden = (act * up).astype(bf16)
        back_up = (back * act).astype(bf16)
        back_gate = (back * up * (sig + act * (1.0 - sig))).astype(bf16)
        return (
            dot(kt_ref[:, at : at + chunk], jnp.concatenate([back_gate, back_up], axis=1)),
            dot(tt_ref[:, at : at + chunk], hidden),
        )

    first, second = part(0)
    for at in range(chunk, k_ref.shape[0], chunk):
        more_first, more_second = part(at)
        first = first + more_first
        second = second + more_second
    direction = orthogonalize([first[:, :LANES], first[:, LANES:], second])
    for j in range(3):
        fresh = moved_on(weights[j], step_ref[0], direction[j], 1 if j == 2 else 0)
        o_ref[j] = encode(fresh, inverse_ref[j])


def tick(step, codes, unit, inverse_unit, prepared):
    return pl.pallas_call(
        functools.partial(tick_body, min(2048, prepared[0].shape[0])),
        out_shape=jax.ShapeDtypeStruct(codes.shape, jnp.int16),
        in_specs=[pl.BlockSpec(memory_space=pltpu.SMEM)] + [on_chip()] * 7,
        out_specs=on_chip(),
        compiler_params=params(),
        name="tick",
    )(step, codes, unit, inverse_unit, *prepared)


def mix_body(rows, x_ref, inverse_ref, gain_ref, row_ref, w_ref, unit_ref, o_ref, part_ref):
    weights = [decode(w_ref[j], unit_ref[j]).astype(bf16) for j in range(3)]
    gate_up = jnp.concatenate(weights[:2], axis=1)
    down = weights[2].T
    norm = jnp.broadcast_to(gain_ref[:, 0:1], (LANES, LANES))
    query = jnp.broadcast_to(gain_ref[:, 1:2], (LANES, LANES))
    scale = row_ref[4:5, :]
    lines = rows // LANES
    for block in range(x_ref.shape[0]):
        inverse = inverse_ref[block]
        pieces = []
        for r in range(lines):
            turned = x_ref[block, r * LANES : (r + 1) * LANES, :].T.astype(f32)
            pieces.append((turned * inverse[r : r + 1] * norm * query).astype(bf16).T)
        both = dot(jnp.concatenate(pieces, axis=0), gate_up)
        gate, up = both[:, :LANES], both[:, LANES:]
        hidden = (gate * (0.5 * jnp.tanh(0.5 * gate) + 0.5) * up).astype(bf16)
        output = dot(hidden, down)
        mixed = (x_ref[block, :rows, :].astype(f32) + scale * output).astype(bf16)
        o_ref[block] = mixed
        wide = mixed.astype(f32)
        wide = wide * wide
        part_ref[block] = jnp.concatenate(
            [jnp.sum(wide[r * LANES : (r + 1) * LANES].T, axis=0, keepdims=True) for r in range(lines)], axis=0
        )


def mix(x, inverse, gains, gain_rows, codes, unit, rows):
    blocks = x.shape[0]
    step = 4
    lines = rows // LANES
    whole = lambda i: (0, 0)
    cube = lambda i: (0, 0, 0)
    moving = lambda i: (i, 0, 0)
    return pl.pallas_call(
        functools.partial(mix_body, rows),
        out_shape=(
            jax.ShapeDtypeStruct((blocks, rows, LANES), bf16),
            jax.ShapeDtypeStruct((blocks, lines, LANES), f32),
        ),
        grid=(blocks // step,),
        in_specs=[
            pl.BlockSpec((step, rows, LANES), moving),
            pl.BlockSpec((step, lines, LANES), moving),
            pl.BlockSpec(gains.shape, whole),
            pl.BlockSpec(gain_rows.shape, whole),
            pl.BlockSpec(codes.shape, cube),
            pl.BlockSpec(unit.shape, cube),
        ],
        out_specs=(
            pl.BlockSpec((step, rows, LANES), moving),
            pl.BlockSpec((step, lines, LANES), moving),
        ),
        compiler_params=params(),
        name="mix",
    )(x, inverse, gains, gain_rows, codes, unit)


def unpack_body(x_ref, o_ref):
    for head in range(x_ref.shape[0]):
        o_ref[:, head * LANES : (head + 1) * LANES] = x_ref[head]


def unpack(x):
    heads, rows, lanes = x.shape
    step = min(rows, 128)
    return pl.pallas_call(
        unpack_body,
        out_shape=jax.ShapeDtypeStruct((rows, heads * lanes), x.dtype),
        grid=(rows // step,),
        in_specs=[pl.BlockSpec((heads, step, lanes), lambda i: (0, i, 0))],
        out_specs=pl.BlockSpec((step, heads * lanes), lambda i: (i, 0)),
        compiler_params=params(),
        name="unpack",
    )(x)


def passed_on(value, index, groups):
    def hop(source):
        return lambda sent: lax.ppermute(sent, "group", [(source, source + 1)])

    return lax.switch(index, [hop(source) for source in range(groups - 1)], value)


def body(tokens, learning_rates, channel_gains, fast_init, step_size, update_table):
    groups = lax.axis_size("group")
    ranks = lax.axis_size("tok")
    me = lax.axis_index("group")
    rows, width = tokens.shape
    layers = fast_init.shape[0]
    lines = rows // LANES

    codes, unit, inverse_unit = setup(fast_init, groups)
    columns = jnp.swapaxes(channel_gains, 1, 2)
    rates = learning_rates.reshape(layers, ranks, lines, LANES)
    stream = lax.all_to_all(pack(tokens), "tok", split_axis=0, concat_axis=0, tiled=True)
    inverse = None

    for layer in range(layers):
        chosen = slice(3 * layer, 3 * layer + 3)
        prepared = prep(stream, inverse, rates[layer], columns[layer], rows)
        if inverse is None:
            inverse = prepared[4]
        prepared = prepared[:4]
        flag = lax.dynamic_index_in_dim(update_table[layer], me, 0, keepdims=False) != 0
        step = step_size[layer]
        layer_unit, layer_inverse = unit[chosen], inverse_unit[chosen]

        def one(index, entering):
            leaving = lax.cond(
                (index == me) & flag,
                lambda held: tick(step, held, layer_unit, layer_inverse, prepared),
                lambda held: held,
                entering,
            )
            received = passed_on(leaving, index, groups)
            return jnp.where(index == me - 1, received, entering)

        entering = lax.fori_loop(
            jnp.maximum(me - 1, 0), jnp.minimum(me + 1, groups - 1), one, codes[chosen]
        )
        stream, partial = mix(
            stream, inverse, columns[layer], channel_gains[layer], entering, layer_unit, rows
        )
        if layer + 1 < layers:
            mine = jnp.sum(lax.all_to_all(partial, "tok", 0, 0, tiled=True), axis=0)
            mine = lax.rsqrt(mine / width + EPSILON)
            inverse = lax.all_to_all(
                jnp.broadcast_to(mine[None], (ranks, lines, LANES)), "tok", 0, 0, tiled=True
            )
    return unpack(lax.all_to_all(stream, "tok", split_axis=0, concat_axis=0, tiled=True))


def solution(mesh):
    in_specs = (
        P(("group", "tok"), None),
        P(None, "group"),
        P(None, None, "tok"),
        P(None, None, "tok", None, None),
        P(None, "tok"),
        P(),
    )
    out_specs = P(("group", "tok"), None)
    return jax.shard_map(body, mesh=mesh, in_specs=in_specs, out_specs=out_specs, check_vma=False)
```

```python
import functools

import jax
import jax.numpy as jnp
from jax import lax
from jax.experimental import pallas as pl
from jax.experimental.pallas import tpu as pltpu
from jax.sharding import PartitionSpec as P

NS_STEPS = 5
MUON_A = 3.4445
MUON_B = -4.775
MUON_C = 2.0315
EPSILON = 1e-06
CODES = 32767.0
LANES = 128

bf16 = jnp.bfloat16
f32 = jnp.float32


def on_chip():
    return pl.BlockSpec(memory_space=pltpu.VMEM)


def params(mebibytes):
    return pltpu.CompilerParams(vmem_limit_bytes=mebibytes * 1024 * 1024)


def dot(left, right):
    return jnp.dot(left, right, preferred_element_type=f32)


def two_parts(value):
    high = value.astype(bf16)
    return high, (value - high.astype(f32)).astype(bf16)


def dot_parts(left, right):
    (lh, ll), (rh, rl) = left, right
    width = rh.shape[1]
    weights = jnp.concatenate(
        [jnp.concatenate([rh, rl], axis=1), jnp.concatenate([rh, jnp.zeros_like(rl)], axis=1)], axis=0
    )
    both = dot(jnp.concatenate([lh, ll], axis=1), weights)
    return both[:, :width] + both[:, width:]


def orthogonalize(gradients):
    current = [
        g * lax.rsqrt(jnp.sum(jnp.sum(g * g, axis=1, keepdims=True), axis=0, keepdims=True) + EPSILON)
        for g in gradients
    ]
    for _ in range(NS_STEPS):
        parts = [two_parts(x) for x in current]
        turned = [two_parts(x.T) for x in current]
        square = [dot_parts(p, t) for p, t in zip(parts, turned)]
        halves = [two_parts(s) for s in square]
        polynom = [MUON_B * s + MUON_C * dot_parts(h, h) for s, h in zip(square, halves)]
        current = [
            MUON_A * x + dot_parts(two_parts(q), p) for x, q, p in zip(current, polynom, parts)
        ]
    return current


def moved_on(weights, step, direction, axis):
    moved = weights + step * direction
    before = jnp.sqrt(jnp.sum(weights * weights, axis=axis, keepdims=True) + EPSILON)
    after = jnp.sqrt(jnp.sum(moved * moved, axis=axis, keepdims=True) + EPSILON)
    return moved * (before / after)


def encode(weights, inverse_unit):
    codes = jnp.clip(jnp.round(weights * inverse_unit), -CODES, CODES)
    return codes.astype(jnp.int32).astype(jnp.int16)


def decode(codes, unit):
    return codes.astype(jnp.int32).astype(f32) * unit


def setup_body(slack, init_ref, code_ref, unit_ref, inverse_ref):
    for index in range(init_ref.shape[0]):
        weights = init_ref[index]
        down = index % 3 == 2
        if down:
            weights = weights.T
        total = jnp.sum(weights * weights, axis=1 if down else 0, keepdims=True) + slack
        unit = jnp.broadcast_to(jnp.sqrt(total) * (1.001 / CODES), weights.shape)
        inverse = 1.0 / unit
        unit_ref[index] = unit
        inverse_ref[index] = inverse
        code_ref[index] = encode(weights, inverse)


def setup(fast_init, groups):
    flat = fast_init.reshape((-1,) + fast_init.shape[-2:])
    return pl.pallas_call(
        functools.partial(setup_body, (groups + 2) * EPSILON),
        out_shape=(
            jax.ShapeDtypeStruct(flat.shape, jnp.int16),
            jax.ShapeDtypeStruct(flat.shape, f32),
            jax.ShapeDtypeStruct(flat.shape, f32),
        ),
        in_specs=[on_chip()],
        out_specs=(on_chip(),) * 3,
        compiler_params=params(20),
        name="setup",
    )(flat)


def pack_body(x_ref, o_ref):
    rows, width = x_ref.shape
    heads = width // LANES
    total = jnp.zeros((rows, LANES), f32)
    for head in range(heads):
        piece = x_ref[:, head * LANES : (head + 1) * LANES]
        o_ref[head, :rows, :] = piece
        wide = piece.astype(f32)
        total = total + wide * wide
    lines = [
        jnp.sum(total[r * LANES : (r + 1) * LANES].T, axis=0, keepdims=True) for r in range(rows // LANES)
    ]
    inverse = lax.rsqrt(jnp.concatenate(lines, axis=0) / width + EPSILON)
    high = inverse.astype(bf16).astype(f32)
    middle = (inverse - high).astype(bf16).astype(f32)
    low = inverse - high - middle
    tail = jnp.concatenate([high, middle, low, jnp.zeros_like(low)], axis=0).astype(bf16)
    for head in range(heads):
        o_ref[head, rows:, :] = tail


def pack(x):
    rows, width = x.shape
    tail = 4 * (rows // LANES)
    return pl.pallas_call(
        pack_body,
        out_shape=jax.ShapeDtypeStruct((width // LANES, rows + tail, LANES), bf16),
        compiler_params=params(20),
        name="pack",
    )(x)


def column_of(lines):
    count = lines.shape[0]
    return jnp.concatenate([lines] * (8 // count), axis=0).T


def prep_body(inverse_inside, rows, *refs):
    if inverse_inside:
        x_ref, rate_ref, gain_ref, early_ref, late_ref, inverse_out = refs
    else:
        x_ref, inverse_ref, rate_ref, gain_ref, early_ref, late_ref = refs
    lines = rows // LANES
    norm, key, value = gain_ref[0:1, :], gain_ref[2:3, :], gain_ref[3:4, :]

    def fill(o_ref):
        for block in range(x_ref.shape[0]):
            if inverse_inside:
                tail = x_ref[block, rows:, :].astype(f32)
                inverse = tail[:lines] + tail[lines : 2 * lines] + tail[2 * lines : 3 * lines]
                inverse_out[block] = inverse
            else:
                inverse = inverse_ref[block]
            inverse = column_of(inverse)
            rate = column_of(rate_ref[block])
            for r in range(lines):
                at = block * rows + r * LANES
                wide = x_ref[block, r * LANES : (r + 1) * LANES, :].astype(f32)
                normed = wide * inverse[:, r : r + 1] * norm
                o_ref[0, at : at + LANES, :] = (normed * key).astype(bf16)
                values = (normed * value).astype(bf16)
                o_ref[1, at : at + LANES, :] = (rate[:, r : r + 1] * values.astype(f32)).astype(bf16)

    half = pl.num_programs(0) // 2

    @pl.when(pl.program_id(0) < half)
    def _():
        fill(early_ref)

    @pl.when(pl.program_id(0) >= half)
    def _():
        fill(late_ref)


def prep(x, inverse, rates, gains, rows):
    blocks, height = x.shape[:2]
    lines = rows // LANES
    step = 4
    half = blocks // step // 2
    pair = jax.ShapeDtypeStruct((2, blocks * rows // 2, LANES), bf16)
    line_spec = pl.BlockSpec((step, lines, LANES), lambda i: (i, 0, 0))
    inside = inverse is None
    shapes = [pair, pair]
    out_specs = [
        pl.BlockSpec((2, step * rows, LANES), lambda i: (0, jnp.minimum(i, half - 1), 0)),
        pl.BlockSpec((2, step * rows, LANES), lambda i: (0, jnp.maximum(i - half, 0), 0)),
    ]
    operands = [x, rates, gains] if inside else [x, inverse, rates, gains]
    in_specs = [pl.BlockSpec((step, height, LANES), lambda i: (i, 0, 0))]
    in_specs += [line_spec] * (len(operands) - 2) + [pl.BlockSpec(gains.shape, lambda i: (0, 0))]
    if inside:
        shapes.append(jax.ShapeDtypeStruct((blocks, lines, LANES), f32))
        out_specs.append(line_spec)
    return pl.pallas_call(
        functools.partial(prep_body, inside, rows),
        out_shape=tuple(shapes),
        grid=(blocks // step,),
        in_specs=in_specs,
        out_specs=tuple(out_specs),
        compiler_params=params(20),
        name="prep",
    )(*operands)


def tick_body(chunk, flag_ref, step_ref, w_ref, unit_ref, inverse_ref, early_ref, late_far, o_ref, kept_ref, late_ref, late_sem):
    updates = flag_ref[0] != 0
    late_in = pltpu.make_async_copy(late_far, late_ref, late_sem)

    @pl.when(updates)
    def _():
        late_in.start()

    kept_ref[...] = w_ref[...]

    @pl.when(jnp.logical_not(updates))
    def _():
        o_ref[...] = w_ref[...]

    @pl.when(updates)
    def _():
        weights = [decode(w_ref[j], unit_ref[j]) for j in range(3)]
        gate_up = jnp.concatenate([weights[0].astype(bf16), weights[1].astype(bf16)], axis=1)
        down = weights[2].astype(bf16)
        over_tokens = functools.partial(
            lax.dot_general, dimension_numbers=(((0,), (0,)), ((), ())), preferred_element_type=f32
        )

        def part(d_ref, at):
            keys = d_ref[0, at : at + chunk, :]
            targets = d_ref[1, at : at + chunk, :]
            both = dot(keys, gate_up)
            back = dot(targets, down)
            gate, up = both[:, :LANES], both[:, LANES:]
            sig = 0.5 * jnp.tanh(0.5 * gate) + 0.5
            act = gate * sig
            hidden = (act * up).astype(bf16)
            back_up = (back * act).astype(bf16)
            back_gate = (back * up * (sig + act * (1.0 - sig))).astype(bf16)
            return (
                over_tokens(keys, jnp.concatenate([back_gate, back_up], axis=1)),
                over_tokens(targets, hidden),
            )

        first, second = part(early_ref, 0)
        for d_ref, begin in ((early_ref, chunk), (late_ref, 0)):
            if d_ref is late_ref:
                late_in.wait()
            for at in range(begin, d_ref.shape[1], chunk):
                more_first, more_second = part(d_ref, at)
                first = first + more_first
                second = second + more_second
        direction = orthogonalize([first[:, :LANES], first[:, LANES:], second])
        for j in range(3):
            fresh = moved_on(weights[j], step_ref[0], direction[j], 1 if j == 2 else 0)
            o_ref[j] = encode(fresh, inverse_ref[j])


def tick(flag, step, codes, unit, inverse_unit, early, late):
    far = pl.BlockSpec(memory_space=pltpu.HBM)
    scalar = pl.BlockSpec(memory_space=pltpu.SMEM)
    shape = jax.ShapeDtypeStruct(codes.shape, jnp.int16)
    return pl.pallas_call(
        functools.partial(tick_body, min(2048, early.shape[1])),
        out_shape=(shape, shape),
        in_specs=[scalar, scalar, on_chip(), on_chip(), on_chip(), on_chip(), far],
        out_specs=(on_chip(), on_chip()),
        scratch_shapes=[
            pltpu.VMEM(late.shape, bf16),
            pltpu.SemaphoreType.DMA,
        ],
        compiler_params=params(24),
        name="tick",
    )(flag, step, codes, unit, inverse_unit, early, late)


def mix_body(rows, x_ref, inverse_ref, gain_ref, w_ref, unit_ref, o_ref, *part_ref):
    weights = [decode(w_ref[j], unit_ref[j]).astype(bf16) for j in range(3)]
    gate_up = jnp.concatenate(weights[:2], axis=1)
    down = weights[2].T
    norm, query, scale = gain_ref[0:1, :], gain_ref[1:2, :], gain_ref[4:5, :]
    lines = rows // LANES
    ones = jnp.ones((8, LANES), bf16)
    for block in range(x_ref.shape[0]):
        inverse = column_of(inverse_ref[block])
        wide = x_ref[block].astype(f32)
        pieces = [
            (wide[r * LANES : (r + 1) * LANES] * inverse[:, r : r + 1] * norm * query).astype(bf16)
            for r in range(lines)
        ]
        both = dot(jnp.concatenate(pieces, axis=0), gate_up)
        gate, up = both[:, :LANES], both[:, LANES:]
        hidden = (gate * (0.5 * jnp.tanh(0.5 * gate) + 0.5) * up).astype(bf16)
        output = dot(hidden, down)
        mixed = (wide + scale * output).astype(bf16)
        o_ref[block] = mixed
        if part_ref:
            square = mixed.astype(f32)
            high, low = two_parts(square * square)
            turned = (((1,), (1,)), ((), ()))
            total = lax.dot_general(ones, high, turned, preferred_element_type=f32) + lax.dot_general(
                ones, low, turned, preferred_element_type=f32
            )
            part_ref[0][block] = jnp.concatenate(
                [total[0:1, r * LANES : (r + 1) * LANES] for r in range(lines)], axis=0
            )


def mix(x, inverse, gains, codes, unit, rows, sums):
    blocks = x.shape[0]
    step = 4
    lines = rows // LANES
    whole = lambda i: (0, 0)
    cube = lambda i: (0, 0, 0)
    moving = lambda i: (i, 0, 0)
    shapes = [jax.ShapeDtypeStruct((blocks, rows, LANES), bf16)]
    out_specs = [pl.BlockSpec((step, rows, LANES), moving)]
    if sums:
        shapes.append(jax.ShapeDtypeStruct((blocks, lines, LANES), f32))
        out_specs.append(pl.BlockSpec((step, lines, LANES), moving))
    return pl.pallas_call(
        functools.partial(mix_body, rows),
        out_shape=tuple(shapes),
        grid=(blocks // step,),
        in_specs=[
            pl.BlockSpec((step, rows, LANES), moving),
            pl.BlockSpec((step, lines, LANES), moving),
            pl.BlockSpec(gains.shape, whole),
            pl.BlockSpec(codes.shape, cube),
            pl.BlockSpec(unit.shape, cube),
        ],
        out_specs=tuple(out_specs),
        compiler_params=params(20),
        name="mix",
    )(x, inverse, gains, codes, unit)


def unpack_body(x_ref, o_ref):
    for head in range(x_ref.shape[0]):
        o_ref[:, head * LANES : (head + 1) * LANES] = x_ref[head]


def unpack(x):
    heads, rows, lanes = x.shape
    step = min(rows, 128)
    return pl.pallas_call(
        unpack_body,
        out_shape=jax.ShapeDtypeStruct((rows, heads * lanes), x.dtype),
        grid=(rows // step,),
        in_specs=[pl.BlockSpec((heads, step, lanes), lambda i: (0, i, 0))],
        out_specs=pl.BlockSpec((step, heads * lanes), lambda i: (i, 0)),
        compiler_params=params(20),
        name="unpack",
    )(x)


def passed_on(value, index, groups):
    def hop(source):
        return lambda sent: lax.ppermute(sent, "group", [(source, source + 1)])

    branches = [hop(source) for source in range(groups - 1)] + [lambda sent: sent]
    return lax.switch(index, branches, value)


def summed_over(value, axis):
    size = lax.axis_size(axis)
    bit = 1
    while bit < size:
        value = value + lax.ppermute(value, axis, [(i, i ^ bit) for i in range(size)])
        bit *= 2
    return value


def body(tokens, learning_rates, channel_gains, fast_init, step_size, update_table):
    groups = lax.axis_size("group")
    ranks = lax.axis_size("tok")
    me = lax.axis_index("group")
    rows, width = tokens.shape
    layers = fast_init.shape[0]
    lines = rows // LANES

    codes, unit, inverse_unit = setup(fast_init, groups)
    rates = learning_rates.reshape(layers, ranks, lines, LANES)
    stream = lax.all_to_all(pack(tokens), "tok", split_axis=0, concat_axis=0, tiled=True)
    inverse = None

    for layer in range(layers):
        chosen = slice(3 * layer, 3 * layer + 3)
        prepared = prep(stream, inverse, rates[layer], channel_gains[layer], rows)
        if inverse is None:
            inverse = prepared[2]
        early = pltpu.with_memory_space_constraint(prepared[0], pltpu.VMEM)
        late = prepared[1]
        flag = lax.dynamic_slice(update_table[layer], (me,), (1,))
        flag = jnp.where(me < groups - 1, flag, 0)
        step = step_size[layer]
        layer_unit, layer_inverse = unit[chosen], inverse_unit[chosen]

        def one(index, held):
            leaving, kept = lax.cond(
                index == me,
                lambda now, _: tick(flag, step, now, layer_unit, layer_inverse, early, late),
                lambda now, before: (now, before),
                *held,
            )
            return passed_on(leaving, index, groups), kept

        first = codes[chosen]
        _, entering = lax.fori_loop(jnp.maximum(me - 1, 0), me + 1, one, (first, first))
        last = layer + 1 == layers
        outcome = mix(stream, inverse, channel_gains[layer], entering, layer_unit, rows, not last)
        stream = outcome[0]
        if not last:
            inverse = lax.rsqrt(summed_over(outcome[1], "tok") / width + EPSILON)
    return unpack(lax.all_to_all(stream, "tok", split_axis=0, concat_axis=0, tiled=True))


def solution(mesh):
    in_specs = (
        P(("group", "tok"), None),
        P(None, "group"),
        P(None, None, "tok"),
        P(None, None, "tok", None, None),
        P(None, "tok"),
        P(),
    )
    out_specs = P(("group", "tok"), None)
    return jax.shard_map(body, mesh=mesh, in_specs=in_specs, out_specs=out_specs, check_vma=False)
```

```python
import functools

import jax
import jax.numpy as jnp
from jax import lax
from jax.experimental import pallas as pl
from jax.experimental.pallas import tpu as pltpu
from jax.sharding import PartitionSpec as P

NS_STEPS = 5
MUON_A = 3.4445
MUON_B = -4.775
MUON_C = 2.0315
EPSILON = 1e-06
CODES = 32767.0
LANES = 128

bf16 = jnp.bfloat16
f32 = jnp.float32


def on_chip():
    return pl.BlockSpec(memory_space=pltpu.VMEM)


def params(mebibytes):
    return pltpu.CompilerParams(vmem_limit_bytes=mebibytes * 1024 * 1024)


def dot(left, right):
    return jnp.dot(left, right, preferred_element_type=f32)


def two_parts(value):
    high = value.astype(bf16)
    return high, (value - high.astype(f32)).astype(bf16)


def dot_parts(left, right):
    (lh, ll), (rh, rl) = left, right
    width = rh.shape[1]
    weights = jnp.concatenate(
        [jnp.concatenate([rh, rl], axis=1), jnp.concatenate([rh, jnp.zeros_like(rl)], axis=1)], axis=0
    )
    both = dot(jnp.concatenate([lh, ll], axis=1), weights)
    return both[:, :width] + both[:, width:]


def orthogonalize(gradients):
    current = [
        g * lax.rsqrt(jnp.sum(jnp.sum(g * g, axis=1, keepdims=True), axis=0, keepdims=True) + EPSILON)
        for g in gradients
    ]
    for _ in range(NS_STEPS):
        parts = [two_parts(x) for x in current]
        turned = [two_parts(x.T) for x in current]
        square = [dot_parts(p, t) for p, t in zip(parts, turned)]
        halves = [two_parts(s) for s in square]
        polynom = [MUON_B * s + MUON_C * dot_parts(h, h) for s, h in zip(square, halves)]
        current = [
            MUON_A * x + dot_parts(two_parts(q), p) for x, q, p in zip(current, polynom, parts)
        ]
    return current


def moved_on(weights, step, direction, axis):
    moved = weights + step * direction
    before = jnp.sqrt(jnp.sum(weights * weights, axis=axis, keepdims=True) + EPSILON)
    after = jnp.sqrt(jnp.sum(moved * moved, axis=axis, keepdims=True) + EPSILON)
    return moved * (before / after)


def encode(weights, inverse_unit):
    codes = jnp.clip(jnp.round(weights * inverse_unit), -CODES, CODES)
    return codes.astype(jnp.int32).astype(jnp.int16)


def decode(codes, unit):
    return codes.astype(jnp.int32).astype(f32) * unit


def setup_body(slack, init_ref, code_ref, unit_ref, inverse_ref):
    for index in range(init_ref.shape[0]):
        weights = init_ref[index]
        down = index % 3 == 2
        if down:
            weights = weights.T
        total = jnp.sum(weights * weights, axis=1 if down else 0, keepdims=True) + slack
        unit = jnp.broadcast_to(jnp.sqrt(total) * (1.001 / CODES), weights.shape)
        inverse = 1.0 / unit
        unit_ref[index] = unit
        inverse_ref[index] = inverse
        code_ref[index] = encode(weights, inverse)


def setup(fast_init, groups):
    flat = fast_init.reshape((-1,) + fast_init.shape[-2:])
    return pl.pallas_call(
        functools.partial(setup_body, (groups + 2) * EPSILON),
        out_shape=(
            jax.ShapeDtypeStruct(flat.shape, jnp.int16),
            jax.ShapeDtypeStruct(flat.shape, f32),
            jax.ShapeDtypeStruct(flat.shape, f32),
        ),
        in_specs=[on_chip()],
        out_specs=(on_chip(),) * 3,
        compiler_params=params(20),
        name="setup",
    )(flat)


def pack_body(x_ref, o_ref):
    rows, width = x_ref.shape
    heads = width // LANES
    total = jnp.zeros((rows, LANES), f32)
    for head in range(heads):
        piece = x_ref[:, head * LANES : (head + 1) * LANES]
        o_ref[head, :rows, :] = piece
        wide = piece.astype(f32)
        total = total + wide * wide
    lines = [
        jnp.sum(total[r * LANES : (r + 1) * LANES].T, axis=0, keepdims=True) for r in range(rows // LANES)
    ]
    inverse = lax.rsqrt(jnp.concatenate(lines, axis=0) / width + EPSILON)
    high = inverse.astype(bf16).astype(f32)
    middle = (inverse - high).astype(bf16).astype(f32)
    low = inverse - high - middle
    tail = jnp.concatenate([high, middle, low, jnp.zeros_like(low)], axis=0).astype(bf16)
    for head in range(heads):
        o_ref[head, rows:, :] = tail


def pack(x):
    rows, width = x.shape
    tail = 4 * (rows // LANES)
    return pl.pallas_call(
        pack_body,
        out_shape=jax.ShapeDtypeStruct((width // LANES, rows + tail, LANES), bf16),
        compiler_params=params(20),
        name="pack",
    )(x)


def column_of(lines):
    count = lines.shape[0]
    return jnp.concatenate([lines] * (8 // count), axis=0).T


def prep_body(inverse_inside, rows, *refs):
    if inverse_inside:
        x_ref, rate_ref, gain_ref, early_ref, late_ref, inverse_out = refs
    else:
        x_ref, inverse_ref, rate_ref, gain_ref, early_ref, late_ref = refs
    lines = rows // LANES
    norm, key, value = gain_ref[0:1, :], gain_ref[2:3, :], gain_ref[3:4, :]

    def fill(o_ref):
        for block in range(x_ref.shape[0]):
            if inverse_inside:
                tail = x_ref[block, rows:, :].astype(f32)
                inverse = tail[:lines] + tail[lines : 2 * lines] + tail[2 * lines : 3 * lines]
                inverse_out[block] = inverse
            else:
                inverse = inverse_ref[block]
            inverse = column_of(inverse)
            rate = column_of(rate_ref[block])
            for r in range(lines):
                at = block * rows + r * LANES
                wide = x_ref[block, r * LANES : (r + 1) * LANES, :].astype(f32)
                normed = wide * inverse[:, r : r + 1] * norm
                o_ref[0, at : at + LANES, :] = (normed * key).astype(bf16)
                values = (normed * value).astype(bf16)
                o_ref[1, at : at + LANES, :] = (rate[:, r : r + 1] * values.astype(f32)).astype(bf16)

    half = pl.num_programs(0) // 2

    @pl.when(pl.program_id(0) < half)
    def _():
        fill(early_ref)

    @pl.when(pl.program_id(0) >= half)
    def _():
        fill(late_ref)


def prep(x, inverse, rates, gains, rows):
    blocks, height = x.shape[:2]
    lines = rows // LANES
    step = 4
    half = blocks // step // 2
    pair = jax.ShapeDtypeStruct((2, blocks * rows // 2, LANES), bf16)
    line_spec = pl.BlockSpec((step, lines, LANES), lambda i: (i, 0, 0))
    inside = inverse is None
    shapes = [pair, pair]
    out_specs = [
        pl.BlockSpec((2, step * rows, LANES), lambda i: (0, jnp.minimum(i, half - 1), 0)),
        pl.BlockSpec((2, step * rows, LANES), lambda i: (0, jnp.maximum(i - half, 0), 0)),
    ]
    operands = [x, rates, gains] if inside else [x, inverse, rates, gains]
    in_specs = [pl.BlockSpec((step, height, LANES), lambda i: (i, 0, 0))]
    in_specs += [line_spec] * (len(operands) - 2) + [pl.BlockSpec(gains.shape, lambda i: (0, 0))]
    if inside:
        shapes.append(jax.ShapeDtypeStruct((blocks, lines, LANES), f32))
        out_specs.append(line_spec)
    return pl.pallas_call(
        functools.partial(prep_body, inside, rows),
        out_shape=tuple(shapes),
        grid=(blocks // step,),
        in_specs=in_specs,
        out_specs=tuple(out_specs),
        compiler_params=params(20),
        name="prep",
    )(*operands)


def tick_body(chunk, flag_ref, step_ref, w_ref, unit_ref, inverse_ref, early_ref, late_far, o_ref, kept_ref, late_ref, late_sem):
    updates = flag_ref[0] != 0
    late_in = pltpu.make_async_copy(late_far, late_ref, late_sem)

    @pl.when(updates)
    def _():
        late_in.start()

    kept_ref[...] = w_ref[...]

    @pl.when(jnp.logical_not(updates))
    def _():
        o_ref[...] = w_ref[...]

    @pl.when(updates)
    def _():
        weights = [decode(w_ref[j], unit_ref[j]) for j in range(3)]
        gate_up = jnp.concatenate([weights[0].astype(bf16), weights[1].astype(bf16)], axis=1)
        down = weights[2].astype(bf16)
        over_tokens = functools.partial(
            lax.dot_general, dimension_numbers=(((0,), (0,)), ((), ())), preferred_element_type=f32
        )

        def part(d_ref, at):
            keys = d_ref[0, at : at + chunk, :]
            targets = d_ref[1, at : at + chunk, :]
            both = dot(keys, gate_up)
            back = dot(targets, down)
            gate, up = both[:, :LANES], both[:, LANES:]
            sig = 0.5 * jnp.tanh(0.5 * gate) + 0.5
            act = gate * sig
            hidden = (act * up).astype(bf16)
            back_up = (back * act).astype(bf16)
            back_gate = (back * up * (sig + act * (1.0 - sig))).astype(bf16)
            return (
                over_tokens(keys, jnp.concatenate([back_gate, back_up], axis=1)),
                over_tokens(targets, hidden),
            )

        first, second = part(early_ref, 0)
        for d_ref, begin in ((early_ref, chunk), (late_ref, 0)):
            if d_ref is late_ref:
                late_in.wait()
            for at in range(begin, d_ref.shape[1], chunk):
                more_first, more_second = part(d_ref, at)
                first = first + more_first
                second = second + more_second
        direction = orthogonalize([first[:, :LANES], first[:, LANES:], second])
        for j in range(3):
            fresh = moved_on(weights[j], step_ref[0], direction[j], 1 if j == 2 else 0)
            o_ref[j] = encode(fresh, inverse_ref[j])


def tick(flag, step, codes, unit, inverse_unit, early, late):
    far = pl.BlockSpec(memory_space=pltpu.HBM)
    scalar = pl.BlockSpec(memory_space=pltpu.SMEM)
    shape = jax.ShapeDtypeStruct(codes.shape, jnp.int16)
    return pl.pallas_call(
        functools.partial(tick_body, min(2048, early.shape[1])),
        out_shape=(shape, shape),
        in_specs=[scalar, scalar, on_chip(), on_chip(), on_chip(), on_chip(), far],
        out_specs=(on_chip(), on_chip()),
        scratch_shapes=[
            pltpu.VMEM(late.shape, bf16),
            pltpu.SemaphoreType.DMA,
        ],
        compiler_params=params(24),
        name="tick",
    )(flag, step, codes, unit, inverse_unit, early, late)


def mix_body(rows, x_ref, inverse_ref, gain_ref, w_ref, unit_ref, o_ref, *part_ref):
    weights = [decode(w_ref[j], unit_ref[j]).astype(bf16) for j in range(3)]
    gate_up = jnp.concatenate(weights[:2], axis=1)
    down = weights[2].T
    query, scale = gain_ref[0:1, :] * gain_ref[1:2, :], gain_ref[4:5, :]
    lines = rows // LANES
    blocks = x_ref.shape[0]
    pieces = []
    for block in range(blocks):
        inverse = column_of(inverse_ref[block])
        for r in range(lines):
            wide = x_ref[block, r * LANES : (r + 1) * LANES, :].astype(f32)
            pieces.append((wide * inverse[:, r : r + 1] * query).astype(bf16))
    both = dot(jnp.concatenate(pieces, axis=0), gate_up)
    gate, up = both[:, :LANES], both[:, LANES:]
    hidden = (gate * (0.5 * jnp.tanh(0.5 * gate) + 0.5) * up).astype(bf16)
    output = dot(hidden, down)
    ones = jnp.ones((8, LANES), bf16)
    turned = (((1,), (1,)), ((), ()))
    for block in range(blocks):
        mixed = (x_ref[block].astype(f32) + scale * output[block * rows : (block + 1) * rows]).astype(bf16)
        o_ref[block] = mixed
        if part_ref:
            square = mixed.astype(f32)
            high, low = two_parts(square * square)
            total = lax.dot_general(ones, high, turned, preferred_element_type=f32) + lax.dot_general(
                ones, low, turned, preferred_element_type=f32
            )
            part_ref[0][block] = jnp.concatenate(
                [total[0:1, r * LANES : (r + 1) * LANES] for r in range(lines)], axis=0
            )


def mix(x, inverse, gains, codes, unit, rows, sums):
    blocks = x.shape[0]
    step = 4
    lines = rows // LANES
    whole = lambda i: (0, 0)
    cube = lambda i: (0, 0, 0)
    moving = lambda i: (i, 0, 0)
    shapes = [jax.ShapeDtypeStruct((blocks, rows, LANES), bf16)]
    out_specs = [pl.BlockSpec((step, rows, LANES), moving)]
    if sums:
        shapes.append(jax.ShapeDtypeStruct((blocks, lines, LANES), f32))
        out_specs.append(pl.BlockSpec((step, lines, LANES), moving))
    return pl.pallas_call(
        functools.partial(mix_body, rows),
        out_shape=tuple(shapes),
        grid=(blocks // step,),
        in_specs=[
            pl.BlockSpec((step, rows, LANES), moving),
            pl.BlockSpec((step, lines, LANES), moving),
            pl.BlockSpec(gains.shape, whole),
            pl.BlockSpec(codes.shape, cube),
            pl.BlockSpec(unit.shape, cube),
        ],
        out_specs=tuple(out_specs),
        compiler_params=params(20),
        name="mix",
    )(x, inverse, gains, codes, unit)


def unpack_body(x_ref, o_ref):
    for head in range(x_ref.shape[0]):
        o_ref[:, head * LANES : (head + 1) * LANES] = x_ref[head]


def unpack(x):
    heads, rows, lanes = x.shape
    step = min(rows, 128)
    return pl.pallas_call(
        unpack_body,
        out_shape=jax.ShapeDtypeStruct((rows, heads * lanes), x.dtype),
        grid=(rows // step,),
        in_specs=[pl.BlockSpec((heads, step, lanes), lambda i: (0, i, 0))],
        out_specs=pl.BlockSpec((step, heads * lanes), lambda i: (i, 0)),
        compiler_params=params(20),
        name="unpack",
    )(x)


def passed_on(value, index, groups):
    def hop(target):
        return lambda sent: lax.ppermute(sent, "group", [(target - 1, target)])

    return lax.switch(index, [lambda sent: sent] + [hop(target) for target in range(1, groups)], value)


def summed_over(value, axis):
    size = lax.axis_size(axis)
    bit = 1
    while bit < size:
        value = value + lax.ppermute(value, axis, [(i, i ^ bit) for i in range(size)])
        bit *= 2
    return value


def body(tokens, learning_rates, channel_gains, fast_init, step_size, update_table):
    groups = lax.axis_size("group")
    ranks = lax.axis_size("tok")
    me = lax.axis_index("group")
    rows, width = tokens.shape
    layers = fast_init.shape[0]
    lines = rows // LANES

    codes, unit, inverse_unit = setup(fast_init, groups)
    rates = learning_rates.reshape(layers, ranks, lines, LANES)
    stream = lax.all_to_all(pack(tokens), "tok", split_axis=0, concat_axis=0, tiled=True)
    inverse = None

    for layer in range(layers):
        chosen = slice(3 * layer, 3 * layer + 3)
        stream = pltpu.with_memory_space_constraint(stream, pltpu.HBM)
        prepared = prep(stream, inverse, rates[layer], channel_gains[layer], rows)
        if inverse is None:
            inverse = prepared[2]
        early = pltpu.with_memory_space_constraint(prepared[0], pltpu.VMEM)
        late = prepared[1]
        flag = lax.dynamic_slice(update_table[layer], (me,), (1,))
        flag = jnp.where(me < groups - 1, flag, 0)
        step = step_size[layer]
        layer_unit, layer_inverse = unit[chosen], inverse_unit[chosen]

        def one(index, held):
            arrived = passed_on(held[0], index, groups)
            return lax.cond(
                index == me,
                lambda now, _: tick(flag, step, now, layer_unit, layer_inverse, early, late),
                lambda now, before: (now, before),
                arrived,
                held[1],
            )

        first = codes[chosen]
        _, entering = lax.fori_loop(me, jnp.minimum(me + 2, groups), one, (first, first))
        last = layer + 1 == layers
        outcome = mix(stream, inverse, channel_gains[layer], entering, layer_unit, rows, not last)
        stream = outcome[0]
        if not last:
            inverse = lax.rsqrt(summed_over(outcome[1], "tok") / width + EPSILON)
    return unpack(lax.all_to_all(stream, "tok", split_axis=0, concat_axis=0, tiled=True))


def solution(mesh):
    in_specs = (
        P(("group", "tok"), None),
        P(None, "group"),
        P(None, None, "tok"),
        P(None, None, "tok", None, None),
        P(None, "tok"),
        P(),
    )
    out_specs = P(("group", "tok"), None)
    return jax.shard_map(body, mesh=mesh, in_specs=in_specs, out_specs=out_specs, check_vma=False)
```

```python
import functools

import jax
import jax.numpy as jnp
from jax import lax
from jax.experimental import pallas as pl
from jax.experimental.pallas import tpu as pltpu
from jax.sharding import PartitionSpec as P

NS_STEPS = 5
MUON_A = 3.4445
MUON_B = -4.775
MUON_C = 2.0315
EPSILON = 1e-06
CODES = 32767.0
LANES = 128

bf16 = jnp.bfloat16
f32 = jnp.float32


def on_chip():
    return pl.BlockSpec(memory_space=pltpu.VMEM)


def params(mebibytes):
    return pltpu.CompilerParams(vmem_limit_bytes=mebibytes * 1024 * 1024)


def dot(left, right):
    return jnp.dot(left, right, preferred_element_type=f32)


def two_parts(value):
    high = value.astype(bf16)
    return high, (value - high.astype(f32)).astype(bf16)


def dot_parts(left, right):
    (lh, ll), (rh, rl) = left, right
    width = rh.shape[1]
    weights = jnp.concatenate(
        [jnp.concatenate([rh, rl], axis=1), jnp.concatenate([rh, jnp.zeros_like(rl)], axis=1)], axis=0
    )
    both = dot(jnp.concatenate([lh, ll], axis=1), weights)
    return both[:, :width] + both[:, width:]


def orthogonalize(gradients):
    current = [
        g * lax.rsqrt(jnp.sum(jnp.sum(g * g, axis=1, keepdims=True), axis=0, keepdims=True) + EPSILON)
        for g in gradients
    ]
    for _ in range(NS_STEPS):
        parts = [two_parts(x) for x in current]
        turned = [two_parts(x.T) for x in current]
        square = [dot_parts(p, t) for p, t in zip(parts, turned)]
        halves = [two_parts(s) for s in square]
        polynom = [MUON_B * s + MUON_C * dot_parts(h, h) for s, h in zip(square, halves)]
        current = [
            MUON_A * x + dot_parts(two_parts(q), p) for x, q, p in zip(current, polynom, parts)
        ]
    return current


def moved_on(weights, step, direction, axis):
    moved = weights + step * direction
    before = jnp.sqrt(jnp.sum(weights * weights, axis=axis, keepdims=True) + EPSILON)
    after = jnp.sqrt(jnp.sum(moved * moved, axis=axis, keepdims=True) + EPSILON)
    return moved * (before / after)


def encode(weights, inverse_unit):
    codes = jnp.clip(jnp.round(weights * inverse_unit), -CODES, CODES)
    return codes.astype(jnp.int32).astype(jnp.int16)


def decode(codes, unit):
    return codes.astype(jnp.int32).astype(f32) * unit


def setup_body(slack, init_ref, code_ref, unit_ref, inverse_ref):
    for index in range(init_ref.shape[0]):
        weights = init_ref[index]
        down = index % 3 == 2
        if down:
            weights = weights.T
        total = jnp.sum(weights * weights, axis=1 if down else 0, keepdims=True) + slack
        unit = jnp.broadcast_to(jnp.sqrt(total) * (1.001 / CODES), weights.shape)
        inverse = 1.0 / unit
        unit_ref[index] = unit
        inverse_ref[index] = inverse
        code_ref[index] = encode(weights, inverse)


def setup(fast_init, groups):
    flat = fast_init.reshape((-1,) + fast_init.shape[-2:])
    return pl.pallas_call(
        functools.partial(setup_body, (groups + 2) * EPSILON),
        out_shape=(
            jax.ShapeDtypeStruct(flat.shape, jnp.int16),
            jax.ShapeDtypeStruct(flat.shape, f32),
            jax.ShapeDtypeStruct(flat.shape, f32),
        ),
        in_specs=[on_chip()],
        out_specs=(on_chip(),) * 3,
        compiler_params=params(20),
        name="setup",
    )(flat)


def pack_body(x_ref, o_ref):
    rows, width = x_ref.shape
    heads = width // LANES
    total = jnp.zeros((rows, LANES), f32)
    for head in range(heads):
        piece = x_ref[:, head * LANES : (head + 1) * LANES]
        o_ref[head, :rows, :] = piece
        wide = piece.astype(f32)
        total = total + wide * wide
    lines = [
        jnp.sum(total[r * LANES : (r + 1) * LANES].T, axis=0, keepdims=True) for r in range(rows // LANES)
    ]
    inverse = lax.rsqrt(jnp.concatenate(lines, axis=0) / width + EPSILON)
    high = inverse.astype(bf16).astype(f32)
    middle = (inverse - high).astype(bf16).astype(f32)
    low = inverse - high - middle
    tail = jnp.concatenate([high, middle, low, jnp.zeros_like(low)], axis=0).astype(bf16)
    for head in range(heads):
        o_ref[head, rows:, :] = tail


def pack(x):
    rows, width = x.shape
    tail = 4 * (rows // LANES)
    return pl.pallas_call(
        pack_body,
        out_shape=jax.ShapeDtypeStruct((width // LANES, rows + tail, LANES), bf16),
        compiler_params=params(20),
        name="pack",
    )(x)


def column_of(lines):
    count = lines.shape[0]
    return jnp.concatenate([lines] * (8 // count), axis=0).T


def prep_body(inverse_inside, rows, *refs):
    if inverse_inside:
        x_ref, rate_ref, gain_ref, early_ref, late_ref, inverse_out = refs
    else:
        x_ref, inverse_ref, rate_ref, gain_ref, early_ref, late_ref = refs
    lines = rows // LANES
    norm, key, value = gain_ref[0:1, :], gain_ref[2:3, :], gain_ref[3:4, :]

    def fill(o_ref):
        for block in range(x_ref.shape[0]):
            if inverse_inside:
                tail = x_ref[block, rows:, :].astype(f32)
                inverse = tail[:lines] + tail[lines : 2 * lines] + tail[2 * lines : 3 * lines]
                inverse_out[block] = inverse
            else:
                inverse = inverse_ref[block]
            inverse = column_of(inverse)
            rate = column_of(rate_ref[block])
            for r in range(lines):
                at = block * rows + r * LANES
                wide = x_ref[block, r * LANES : (r + 1) * LANES, :].astype(f32)
                normed = wide * inverse[:, r : r + 1] * norm
                o_ref[0, at : at + LANES, :] = (normed * key).astype(bf16)
                values = (normed * value).astype(bf16)
                o_ref[1, at : at + LANES, :] = (rate[:, r : r + 1] * values.astype(f32)).astype(bf16)

    half = pl.num_programs(0) // 2

    @pl.when(pl.program_id(0) < half)
    def _():
        fill(early_ref)

    @pl.when(pl.program_id(0) >= half)
    def _():
        fill(late_ref)


def prep(x, inverse, rates, gains, rows):
    blocks, height = x.shape[:2]
    lines = rows // LANES
    step = 8
    half = blocks // step // 2
    pair = jax.ShapeDtypeStruct((2, blocks * rows // 2, LANES), bf16)
    line_spec = pl.BlockSpec((step, lines, LANES), lambda i: (i, 0, 0))
    inside = inverse is None
    shapes = [pair, pair]
    out_specs = [
        pl.BlockSpec((2, step * rows, LANES), lambda i: (0, jnp.minimum(i, half - 1), 0)),
        pl.BlockSpec((2, step * rows, LANES), lambda i: (0, jnp.maximum(i - half, 0), 0)),
    ]
    operands = [x, rates, gains] if inside else [x, inverse, rates, gains]
    in_specs = [pl.BlockSpec((step, height, LANES), lambda i: (i, 0, 0))]
    in_specs += [line_spec] * (len(operands) - 2) + [pl.BlockSpec(gains.shape, lambda i: (0, 0))]
    if inside:
        shapes.append(jax.ShapeDtypeStruct((blocks, lines, LANES), f32))
        out_specs.append(line_spec)
    return pl.pallas_call(
        functools.partial(prep_body, inside, rows),
        out_shape=tuple(shapes),
        grid=(blocks // step,),
        in_specs=in_specs,
        out_specs=tuple(out_specs),
        compiler_params=params(40),
        name="prep",
    )(*operands)


def tick_body(chunk, flag_ref, step_ref, w_ref, unit_ref, inverse_ref, early_ref, late_far, o_ref, kept_ref, late_ref, late_sem):
    updates = flag_ref[0] != 0
    late_in = pltpu.make_async_copy(late_far, late_ref, late_sem)

    @pl.when(updates)
    def _():
        late_in.start()

    kept_ref[...] = w_ref[...]

    @pl.when(jnp.logical_not(updates))
    def _():
        o_ref[...] = w_ref[...]

    @pl.when(updates)
    def _():
        weights = [decode(w_ref[j], unit_ref[j]) for j in range(3)]
        gate_up = jnp.concatenate(
            [0.5 * weights[0].astype(bf16).astype(f32), 0.5 * weights[1].astype(bf16).astype(f32)], axis=1
        ).astype(bf16)
        down = weights[2].astype(bf16)
        over_tokens = functools.partial(
            lax.dot_general, dimension_numbers=(((0,), (0,)), ((), ())), preferred_element_type=f32
        )

        def part(d_ref, at):
            keys = d_ref[0, at : at + chunk, :]
            targets = d_ref[1, at : at + chunk, :]
            both = dot(keys, gate_up)
            back = dot(targets, down)
            half, half_up = both[:, :LANES], both[:, LANES:]
            bent = jnp.tanh(half)
            slope = half * bent
            act = half + slope
            hidden = (act * half_up).astype(bf16)
            back_up = (back * act).astype(bf16)
            rise = (1.0 + bent) * (1.0 + (half - slope))
            back_gate = (back * half_up * rise).astype(bf16)
            return (
                over_tokens(keys, jnp.concatenate([back_gate, back_up], axis=1)),
                over_tokens(targets, hidden),
            )

        first, second = part(early_ref, 0)
        for d_ref, begin in ((early_ref, chunk), (late_ref, 0)):
            if d_ref is late_ref:
                late_in.wait()
            for at in range(begin, d_ref.shape[1], chunk):
                more_first, more_second = part(d_ref, at)
                first = first + more_first
                second = second + more_second
        direction = orthogonalize([first[:, :LANES], first[:, LANES:], 2.0 * second])
        for j in range(3):
            fresh = moved_on(weights[j], step_ref[0], direction[j], 1 if j == 2 else 0)
            o_ref[j] = encode(fresh, inverse_ref[j])


def tick(flag, step, codes, unit, inverse_unit, early, late):
    far = pl.BlockSpec(memory_space=pltpu.HBM)
    scalar = pl.BlockSpec(memory_space=pltpu.SMEM)
    shape = jax.ShapeDtypeStruct(codes.shape, jnp.int16)
    return pl.pallas_call(
        functools.partial(tick_body, min(2048, early.shape[1])),
        out_shape=(shape, shape),
        in_specs=[scalar, scalar, on_chip(), on_chip(), on_chip(), on_chip(), far],
        out_specs=(on_chip(), on_chip()),
        scratch_shapes=[
            pltpu.VMEM(late.shape, bf16),
            pltpu.SemaphoreType.DMA,
        ],
        compiler_params=params(24),
        name="tick",
    )(flag, step, codes, unit, inverse_unit, early, late)


def mix_body(rows, x_ref, inverse_ref, gain_ref, w_ref, unit_ref, _, o_ref, *part_ref):
    weights = [decode(w_ref[j], unit_ref[j]).astype(bf16) for j in range(3)]
    gate_up = jnp.concatenate(weights[:2], axis=1)
    down = weights[2].T
    query, scale = gain_ref[0:1, :] * gain_ref[1:2, :], gain_ref[4:5, :]
    lines = rows // LANES
    blocks = x_ref.shape[0]
    pieces = []
    for block in range(blocks):
        inverse = column_of(inverse_ref[block])
        for r in range(lines):
            wide = x_ref[block, r * LANES : (r + 1) * LANES, :].astype(f32)
            pieces.append((wide * inverse[:, r : r + 1] * query).astype(bf16))
    both = dot(jnp.concatenate(pieces, axis=0), gate_up)
    gate, up = both[:, :LANES], both[:, LANES:]
    hidden = (gate * (0.5 * jnp.tanh(0.5 * gate) + 0.5) * up).astype(bf16)
    output = dot(hidden, down)
    ones = jnp.ones((8, LANES), bf16)
    turned = (((1,), (1,)), ((), ()))
    for block in range(blocks):
        mixed = (x_ref[block].astype(f32) + scale * output[block * rows : (block + 1) * rows]).astype(bf16)
        o_ref[block] = mixed
        if part_ref:
            square = mixed.astype(f32)
            high, low = two_parts(square * square)
            total = lax.dot_general(ones, high, turned, preferred_element_type=f32) + lax.dot_general(
                ones, low, turned, preferred_element_type=f32
            )
            part_ref[0][block] = jnp.concatenate(
                [total[0:1, r * LANES : (r + 1) * LANES] for r in range(lines)], axis=0
            )


def mix(x, inverse, gains, codes, unit, after, rows, sums):
    blocks = x.shape[0]
    step = 8
    lines = rows // LANES
    whole = lambda i: (0, 0)
    cube = lambda i: (0, 0, 0)
    moving = lambda i: (i, 0, 0)
    shapes = [(pltpu.HBM if sums else jax.ShapeDtypeStruct)((blocks, rows, LANES), bf16)]
    out_specs = [pl.BlockSpec((step, rows, LANES), moving)]
    if sums:
        shapes.append(jax.ShapeDtypeStruct((blocks, lines, LANES), f32))
        out_specs.append(pl.BlockSpec((step, lines, LANES), moving))
    return pl.pallas_call(
        functools.partial(mix_body, rows),
        out_shape=tuple(shapes),
        grid=(blocks // step,),
        in_specs=[
            pl.BlockSpec((step, rows, LANES), moving),
            pl.BlockSpec((step, lines, LANES), moving),
            pl.BlockSpec(gains.shape, whole),
            pl.BlockSpec(codes.shape, cube),
            pl.BlockSpec(unit.shape, cube),
            pl.BlockSpec(memory_space=pl.ANY),
        ],
        out_specs=tuple(out_specs),
        compiler_params=params(40),
        name="mix",
    )(x, inverse, gains, codes, unit, after)


def unpack_body(x_ref, o_ref):
    for head in range(x_ref.shape[0]):
        o_ref[:, head * LANES : (head + 1) * LANES] = x_ref[head]


def unpack(x):
    heads, rows, lanes = x.shape
    step = min(rows, 128)
    return pl.pallas_call(
        unpack_body,
        out_shape=jax.ShapeDtypeStruct((rows, heads * lanes), x.dtype),
        grid=(rows // step,),
        in_specs=[pl.BlockSpec((heads, step, lanes), lambda i: (0, i, 0))],
        out_specs=pl.BlockSpec((step, heads * lanes), lambda i: (i, 0)),
        compiler_params=params(20),
        name="unpack",
    )(x)


def passed_on(value, index, groups):
    def hop(target):
        return lambda sent: lax.ppermute(sent, "group", [(target - 1, target)])

    return lax.switch(index, [lambda sent: sent] + [hop(target) for target in range(1, groups)], value)


def held_back(state, me, groups):
    row = 4
    targets = list(range(row - 1, groups - row - 1, row))
    if not targets:
        return jnp.zeros((8, LANES), f32)
    source = targets[-1] + row

    def release(state):
        seed = state[0, :8, :].astype(f32)
        return sum(lax.ppermute(seed, "group", [(source, target)]) for target in targets)

    joins = functools.reduce(jnp.logical_or, [me == group for group in targets + [source]])
    return lax.cond(joins, release, lambda state: jnp.zeros((8, LANES), f32), state)


def summed_over(value, axis):
    size = lax.axis_size(axis)
    bit = 1
    while bit < size:
        value = value + lax.ppermute(value, axis, [(i, i ^ bit) for i in range(size)])
        bit *= 2
    return value


def body(tokens, learning_rates, channel_gains, fast_init, step_size, update_table):
    groups = lax.axis_size("group")
    ranks = lax.axis_size("tok")
    me = lax.axis_index("group")
    rows, width = tokens.shape
    layers = fast_init.shape[0]
    lines = rows // LANES

    codes, unit, inverse_unit = setup(fast_init, groups)
    rates = learning_rates.reshape(layers, ranks, lines, LANES)
    stream = lax.all_to_all(pack(tokens), "tok", split_axis=0, concat_axis=0, tiled=True)
    inverse = None

    for layer in range(layers):
        chosen = slice(3 * layer, 3 * layer + 3)
        stream = pltpu.with_memory_space_constraint(stream, pltpu.HBM)
        prepared = prep(stream, inverse, rates[layer], channel_gains[layer], rows)
        if inverse is None:
            inverse = prepared[2]
        early = pltpu.with_memory_space_constraint(prepared[0], pltpu.VMEM)
        late = prepared[1]
        flag = lax.dynamic_slice(update_table[layer], (me,), (1,))
        flag = jnp.where(me < groups - 1, flag, 0)
        step = step_size[layer]
        layer_unit, layer_inverse = unit[chosen], inverse_unit[chosen]

        def one(index, held):
            arrived = passed_on(held[0], index, groups)
            return lax.cond(
                index == me,
                lambda now, _: tick(flag, step, now, layer_unit, layer_inverse, early, late),
                lambda now, before: (now, before),
                arrived,
                held[1],
            )

        first = codes[chosen]
        _, entering = lax.fori_loop(me, jnp.minimum(me + 2, groups), one, (first, first))
        last = layer + 1 == layers
        after = held_back(entering, me, groups) if last else jnp.zeros((8, LANES), f32)
        outcome = mix(stream, inverse, channel_gains[layer], entering, layer_unit, after, rows, not last)
        stream = outcome[0]
        if not last:
            inverse = lax.rsqrt(summed_over(outcome[1], "tok") / width + EPSILON)
    return unpack(lax.all_to_all(stream, "tok", split_axis=0, concat_axis=0, tiled=True))


def solution(mesh):
    in_specs = (
        P(("group", "tok"), None),
        P(None, "group"),
        P(None, None, "tok"),
        P(None, None, "tok", None, None),
        P(None, "tok"),
        P(),
    )
    out_specs = P(("group", "tok"), None)
    return jax.shard_map(body, mesh=mesh, in_specs=in_specs, out_specs=out_specs, check_vma=False)
```

```python
import functools

import jax
import jax.numpy as jnp
from jax import lax
from jax.experimental import pallas as pl
from jax.experimental.pallas import tpu as pltpu
from jax.sharding import PartitionSpec as P

NS_STEPS = 5
MUON_A = 3.4445
MUON_B = -4.775
MUON_C = 2.0315
EPSILON = 1e-06
CODES = 32767.0
LANES = 128

bf16 = jnp.bfloat16
f32 = jnp.float32


def on_chip():
    return pl.BlockSpec(memory_space=pltpu.VMEM)


def params(mebibytes):
    return pltpu.CompilerParams(vmem_limit_bytes=mebibytes * 1024 * 1024)


def dot(left, right):
    return jnp.dot(left, right, preferred_element_type=f32)


def two_parts(value):
    high = value.astype(bf16)
    return high, (value - high.astype(f32)).astype(bf16)


def dot_parts(left, right):
    (lh, ll), (rh, rl) = left, right
    width = rh.shape[1]
    weights = jnp.concatenate(
        [jnp.concatenate([rh, rl], axis=1), jnp.concatenate([rh, jnp.zeros_like(rl)], axis=1)], axis=0
    )
    both = dot(jnp.concatenate([lh, ll], axis=1), weights)
    return both[:, :width] + both[:, width:]


def gram(parts):
    high, low = parts
    rows = jnp.concatenate(
        [jnp.concatenate([high, high], axis=1), jnp.concatenate([low, jnp.zeros_like(low)], axis=1)], axis=0
    )
    both = lax.dot_general(
        jnp.concatenate([high, low], axis=1), rows, (((1,), (1,)), ((), ())), preferred_element_type=f32
    )
    return both[:, : high.shape[0]] + both[:, high.shape[0] :]


def orthogonalize(gradients):
    current = [
        g * lax.rsqrt(jnp.sum(jnp.sum(g * g, axis=1, keepdims=True), axis=0, keepdims=True) + EPSILON)
        for g in gradients
    ]
    for _ in range(NS_STEPS):
        parts = [two_parts(x) for x in current]
        square = [gram(p) for p in parts]
        halves = [two_parts(s) for s in square]
        polynom = [MUON_B * s + MUON_C * dot_parts(h, h) for s, h in zip(square, halves)]
        current = [
            MUON_A * x + dot_parts(two_parts(q), p) for x, q, p in zip(current, polynom, parts)
        ]
    return current


def moved_on(weights, step, direction, axis):
    moved = weights + step * direction
    before = jnp.sqrt(jnp.sum(weights * weights, axis=axis, keepdims=True) + EPSILON)
    after = jnp.sqrt(jnp.sum(moved * moved, axis=axis, keepdims=True) + EPSILON)
    return moved * (before / after)


def encode(weights, inverse_unit):
    codes = jnp.clip(jnp.round(weights * inverse_unit), -CODES, CODES)
    return codes.astype(jnp.int32).astype(jnp.int16)


def decode(codes, unit):
    return codes.astype(jnp.int32).astype(f32) * unit


def setup_body(slack, init_ref, code_ref, unit_ref, inverse_ref):
    for index in range(init_ref.shape[0]):
        weights = init_ref[index]
        down = index % 3 == 2
        if down:
            weights = weights.T
        total = jnp.sum(weights * weights, axis=1 if down else 0, keepdims=True) + slack
        unit = jnp.broadcast_to(jnp.sqrt(total) * (1.001 / CODES), weights.shape)
        inverse = 1.0 / unit
        unit_ref[index] = unit
        inverse_ref[index] = inverse
        code_ref[index] = encode(weights, inverse)


def setup(fast_init, groups):
    flat = fast_init.reshape((-1,) + fast_init.shape[-2:])
    return pl.pallas_call(
        functools.partial(setup_body, (groups + 2) * EPSILON),
        out_shape=(
            jax.ShapeDtypeStruct(flat.shape, jnp.int16),
            jax.ShapeDtypeStruct(flat.shape, f32),
            jax.ShapeDtypeStruct(flat.shape, f32),
        ),
        in_specs=[on_chip()],
        out_specs=(on_chip(),) * 3,
        compiler_params=params(20),
        name="setup",
    )(flat)


def pack_body(x_ref, o_ref):
    rows, width = x_ref.shape
    heads = width // LANES
    total = jnp.zeros((rows, LANES), f32)
    for head in range(heads):
        piece = x_ref[:, head * LANES : (head + 1) * LANES]
        o_ref[head, :rows, :] = piece
        wide = piece.astype(f32)
        total = total + wide * wide
    lines = [
        jnp.sum(total[r * LANES : (r + 1) * LANES].T, axis=0, keepdims=True) for r in range(rows // LANES)
    ]
    inverse = lax.rsqrt(jnp.concatenate(lines, axis=0) / width + EPSILON)
    high = inverse.astype(bf16).astype(f32)
    middle = (inverse - high).astype(bf16).astype(f32)
    low = inverse - high - middle
    tail = jnp.concatenate([high, middle, low, jnp.zeros_like(low)], axis=0).astype(bf16)
    for head in range(heads):
        o_ref[head, rows:, :] = tail


def pack(x):
    rows, width = x.shape
    tail = 4 * (rows // LANES)
    return pl.pallas_call(
        pack_body,
        out_shape=jax.ShapeDtypeStruct((width // LANES, rows + tail, LANES), bf16),
        compiler_params=params(20),
        name="pack",
    )(x)


def column_of(lines):
    count = lines.shape[0]
    return jnp.concatenate([lines] * (8 // count), axis=0).T


def prep_body(inverse_inside, rows, *refs):
    if inverse_inside:
        x_ref, rate_ref, gain_ref, early_ref, late_ref, inverse_out = refs
    else:
        x_ref, inverse_ref, rate_ref, gain_ref, early_ref, late_ref = refs
    lines = rows // LANES
    norm, key, value = gain_ref[0:1, :], gain_ref[2:3, :], gain_ref[3:4, :]

    def fill(o_ref):
        for block in range(x_ref.shape[0]):
            if inverse_inside:
                tail = x_ref[block, rows:, :].astype(f32)
                inverse = tail[:lines] + tail[lines : 2 * lines] + tail[2 * lines : 3 * lines]
                inverse_out[block] = inverse
            else:
                inverse = inverse_ref[block]
            inverse = column_of(inverse)
            rate = column_of(rate_ref[block])
            for r in range(lines):
                at = block * rows + r * LANES
                wide = x_ref[block, r * LANES : (r + 1) * LANES, :].astype(f32)
                normed = wide * inverse[:, r : r + 1] * norm
                o_ref[0, at : at + LANES, :] = (normed * key).astype(bf16)
                values = (normed * value).astype(bf16)
                o_ref[1, at : at + LANES, :] = (rate[:, r : r + 1] * values.astype(f32)).astype(bf16)

    half = pl.num_programs(0) // 2

    @pl.when(pl.program_id(0) < half)
    def _():
        fill(early_ref)

    @pl.when(pl.program_id(0) >= half)
    def _():
        fill(late_ref)


def prep(x, inverse, rates, gains, rows):
    blocks, height = x.shape[:2]
    lines = rows // LANES
    step = 8
    half = blocks // step // 2
    pair = jax.ShapeDtypeStruct((2, blocks * rows // 2, LANES), bf16)
    line_spec = pl.BlockSpec((step, lines, LANES), lambda i: (i, 0, 0))
    inside = inverse is None
    shapes = [pair, pair]
    out_specs = [
        pl.BlockSpec((2, step * rows, LANES), lambda i: (0, jnp.minimum(i, half - 1), 0)),
        pl.BlockSpec((2, step * rows, LANES), lambda i: (0, jnp.maximum(i - half, 0), 0)),
    ]
    operands = [x, rates, gains] if inside else [x, inverse, rates, gains]
    in_specs = [pl.BlockSpec((step, height, LANES), lambda i: (i, 0, 0))]
    in_specs += [line_spec] * (len(operands) - 2) + [pl.BlockSpec(gains.shape, lambda i: (0, 0))]
    if inside:
        shapes.append(jax.ShapeDtypeStruct((blocks, lines, LANES), f32))
        out_specs.append(line_spec)
    return pl.pallas_call(
        functools.partial(prep_body, inside, rows),
        out_shape=tuple(shapes),
        grid=(blocks // step,),
        in_specs=in_specs,
        out_specs=tuple(out_specs),
        compiler_params=params(40),
        name="prep",
    )(*operands)


def tick_body(chunk, flag_ref, step_ref, w_ref, unit_ref, inverse_ref, early_ref, late_far, o_ref, kept_ref, late_ref, late_sem):
    updates = flag_ref[0] != 0
    late_in = pltpu.make_async_copy(late_far, late_ref, late_sem)

    @pl.when(updates)
    def _():
        late_in.start()


    @pl.when(jnp.logical_not(updates))
    def _():
        o_ref[...] = w_ref[...]
        kept_ref[...] = w_ref[...]

    @pl.when(updates)
    def _():
        weights = [decode(w_ref[j], unit_ref[j]) for j in range(3)]
        gate_up = jnp.concatenate(
            [0.5 * weights[0].astype(bf16).astype(f32), 0.5 * weights[1].astype(bf16).astype(f32)], axis=1
        ).astype(bf16)
        down = weights[2].astype(bf16)
        over_tokens = functools.partial(
            lax.dot_general, dimension_numbers=(((0,), (0,)), ((), ())), preferred_element_type=f32
        )

        def part(d_ref, at):
            keys = d_ref[0, at : at + chunk, :]
            targets = d_ref[1, at : at + chunk, :]
            both = dot(keys, gate_up)
            back = dot(targets, down)
            half, half_up = both[:, :LANES], both[:, LANES:]
            bent = jnp.tanh(half)
            slope = half * bent
            act = half + slope
            hidden = (act * half_up).astype(bf16)
            back_up = (back * act).astype(bf16)
            rise = (1.0 + bent) * (1.0 + (half - slope))
            back_gate = (back * half_up * rise).astype(bf16)
            return (
                over_tokens(keys, jnp.concatenate([back_gate, back_up], axis=1)),
                over_tokens(targets, hidden),
            )

        first, second = part(early_ref, 0)
        for d_ref, begin in ((early_ref, chunk), (late_ref, 0)):
            if d_ref is late_ref:
                late_in.wait()
            for at in range(begin, d_ref.shape[1], chunk):
                more_first, more_second = part(d_ref, at)
                first = first + more_first
                second = second + more_second
        direction = orthogonalize([first[:, :LANES], first[:, LANES:], 2.0 * second])
        for j in range(3):
            fresh = moved_on(weights[j], step_ref[0], direction[j], 1 if j == 2 else 0)
            o_ref[j] = encode(fresh, inverse_ref[j])
            kept_ref[j] = w_ref[j]


def tick(flag, step, codes, unit, inverse_unit, early, late):
    far = pl.BlockSpec(memory_space=pltpu.HBM)
    scalar = pl.BlockSpec(memory_space=pltpu.SMEM)
    shape = jax.ShapeDtypeStruct(codes.shape, jnp.int16)
    return pl.pallas_call(
        functools.partial(tick_body, min(2048, early.shape[1])),
        out_shape=(shape, shape),
        in_specs=[scalar, scalar, on_chip(), on_chip(), on_chip(), on_chip(), far],
        out_specs=(on_chip(), on_chip()),
        scratch_shapes=[
            pltpu.VMEM(late.shape, bf16),
            pltpu.SemaphoreType.DMA,
        ],
        compiler_params=params(24),
        name="tick",
    )(flag, step, codes, unit, inverse_unit, early, late)


def mix_body(rows, x_ref, inverse_ref, gain_ref, w_ref, unit_ref, _, o_ref, *part_ref):
    weights = [decode(w_ref[j], unit_ref[j]).astype(bf16) for j in range(3)]
    gate_up = jnp.concatenate(weights[:2], axis=1)
    down = weights[2].T
    query, scale = gain_ref[0:1, :] * gain_ref[1:2, :], gain_ref[4:5, :]
    lines = rows // LANES
    blocks = x_ref.shape[0]
    pieces = []
    for block in range(blocks):
        inverse = column_of(inverse_ref[block])
        for r in range(lines):
            wide = x_ref[block, r * LANES : (r + 1) * LANES, :].astype(f32)
            pieces.append((wide * inverse[:, r : r + 1] * query).astype(bf16))
    both = dot(jnp.concatenate(pieces, axis=0), gate_up)
    gate, up = both[:, :LANES], both[:, LANES:]
    hidden = (gate * (0.5 * jnp.tanh(0.5 * gate) + 0.5) * up).astype(bf16)
    output = dot(hidden, down)
    ones = jnp.ones((2 * LANES, LANES), bf16)
    own = lax.broadcasted_iota(jnp.int32, (LANES, LANES), 0) == lax.broadcasted_iota(jnp.int32, (LANES, LANES), 1)
    for block in range(blocks):
        mixed = (x_ref[block].astype(f32) + scale * output[block * rows : (block + 1) * rows]).astype(bf16)
        o_ref[block] = mixed
        if part_ref:
            square = mixed.astype(f32)
            total = dot(jnp.concatenate(two_parts(square * square), axis=1), ones)
            part_ref[0][block] = jnp.concatenate(
                [
                    jnp.sum(jnp.where(own, total[r * LANES : (r + 1) * LANES], 0.0), axis=0, keepdims=True)
                    for r in range(lines)
                ],
                axis=0,
            )


def mix(x, inverse, gains, codes, unit, after, rows, sums):
    blocks = x.shape[0]
    step = 8
    lines = rows // LANES
    whole = lambda i: (0, 0)
    cube = lambda i: (0, 0, 0)
    moving = lambda i: (i, 0, 0)
    shapes = [(pltpu.HBM if sums else jax.ShapeDtypeStruct)((blocks, rows, LANES), bf16)]
    out_specs = [pl.BlockSpec((step, rows, LANES), moving)]
    if sums:
        shapes.append(jax.ShapeDtypeStruct((blocks, lines, LANES), f32))
        out_specs.append(pl.BlockSpec((step, lines, LANES), moving))
    return pl.pallas_call(
        functools.partial(mix_body, rows),
        out_shape=tuple(shapes),
        grid=(blocks // step,),
        in_specs=[
            pl.BlockSpec((step, rows, LANES), moving),
            pl.BlockSpec((step, lines, LANES), moving),
            pl.BlockSpec(gains.shape, whole),
            pl.BlockSpec(codes.shape, cube),
            pl.BlockSpec(unit.shape, cube),
            pl.BlockSpec(memory_space=pl.ANY),
        ],
        out_specs=tuple(out_specs),
        compiler_params=params(40),
        name="mix",
    )(x, inverse, gains, codes, unit, after)


def unpack_body(x_ref, o_ref):
    for head in range(x_ref.shape[0]):
        o_ref[:, head * LANES : (head + 1) * LANES] = x_ref[head]


def unpack(x):
    heads, rows, lanes = x.shape
    step = min(rows, 128)
    return pl.pallas_call(
        unpack_body,
        out_shape=jax.ShapeDtypeStruct((rows, heads * lanes), x.dtype),
        grid=(rows // step,),
        in_specs=[pl.BlockSpec((heads, step, lanes), lambda i: (0, i, 0))],
        out_specs=pl.BlockSpec((step, heads * lanes), lambda i: (i, 0)),
        compiler_params=params(20),
        name="unpack",
    )(x)


def passed_on(value, index, groups):
    def hop(target):
        return lambda sent: lax.ppermute(sent, "group", [(target - 1, target)])

    return lax.switch(index, [lambda sent: sent] + [hop(target) for target in range(1, groups)], value)


def held_back(state, me, groups):
    row = 4
    targets = list(range(row - 1, groups - row - 1, row))
    if not targets:
        return jnp.zeros((8, LANES), f32)
    source = targets[-1] + row

    def release(state):
        seed = state[0, :8, :].astype(f32)
        return sum(lax.ppermute(seed, "group", [(source, target)]) for target in targets)

    joins = functools.reduce(jnp.logical_or, [me == group for group in targets + [source]])
    return lax.cond(joins, release, lambda state: jnp.zeros((8, LANES), f32), state)


def summed_over(value, axis):
    size = lax.axis_size(axis)
    bit = 1
    while bit < size:
        value = value + lax.ppermute(value, axis, [(i, i ^ bit) for i in range(size)])
        bit *= 2
    return value


def body(tokens, learning_rates, channel_gains, fast_init, step_size, update_table):
    groups = lax.axis_size("group")
    ranks = lax.axis_size("tok")
    me = lax.axis_index("group")
    rows, width = tokens.shape
    layers = fast_init.shape[0]
    lines = rows // LANES

    codes, unit, inverse_unit = setup(fast_init, groups)
    rates = learning_rates.reshape(layers, ranks, lines, LANES)
    stream = lax.all_to_all(pack(tokens), "tok", split_axis=0, concat_axis=0, tiled=True)
    inverse = None

    for layer in range(layers):
        chosen = slice(3 * layer, 3 * layer + 3)
        stream = pltpu.with_memory_space_constraint(stream, pltpu.HBM)
        prepared = prep(stream, inverse, rates[layer], channel_gains[layer], rows)
        if inverse is None:
            inverse = prepared[2]
        early = pltpu.with_memory_space_constraint(prepared[0], pltpu.VMEM)
        late = prepared[1]
        flag = lax.dynamic_slice(update_table[layer], (me,), (1,))
        flag = jnp.where(me < groups - 1, flag, 0)
        step = step_size[layer]
        layer_unit, layer_inverse = unit[chosen], inverse_unit[chosen]

        def one(index, held):
            arrived = passed_on(held[0], index, groups)
            return lax.cond(
                index == me,
                lambda now, _: tick(flag, step, now, layer_unit, layer_inverse, early, late),
                lambda now, before: (now, before),
                arrived,
                held[1],
            )

        first = codes[chosen]
        _, entering = lax.fori_loop(me, jnp.minimum(me + 2, groups), one, (first, first))
        last = layer + 1 == layers
        after = held_back(entering, me, groups) if last else jnp.zeros((8, LANES), f32)
        outcome = mix(stream, inverse, channel_gains[layer], entering, layer_unit, after, rows, not last)
        stream = outcome[0]
        if not last:
            inverse = lax.rsqrt(summed_over(outcome[1], "tok") / width + EPSILON)
    return unpack(lax.all_to_all(stream, "tok", split_axis=0, concat_axis=0, tiled=True))


def solution(mesh):
    in_specs = (
        P(("group", "tok"), None),
        P(None, "group"),
        P(None, None, "tok"),
        P(None, None, "tok", None, None),
        P(None, "tok"),
        P(),
    )
    out_specs = P(("group", "tok"), None)
    return jax.shard_map(body, mesh=mesh, in_specs=in_specs, out_specs=out_specs, check_vma=False)
```

```python
import functools

import jax
import jax.numpy as jnp
from jax import lax
from jax.experimental import pallas as pl
from jax.experimental.pallas import tpu as pltpu
from jax.sharding import PartitionSpec as P

NS_STEPS = 5
MUON_A = 3.4445
MUON_B = -4.775
MUON_C = 2.0315
EPSILON = 1e-06
CODES = 32767.0
LANES = 128

bf16 = jnp.bfloat16
f32 = jnp.float32


def on_chip():
    return pl.BlockSpec(memory_space=pltpu.VMEM)


def params(mebibytes):
    return pltpu.CompilerParams(vmem_limit_bytes=mebibytes * 1024 * 1024)


def dot(left, right):
    return jnp.dot(left, right, preferred_element_type=f32)


def two_parts(value):
    high = value.astype(bf16)
    return high, (value - high.astype(f32)).astype(bf16)


def dot_parts(left, right):
    (lh, ll), (rh, rl) = left, right
    width = rh.shape[1]
    weights = jnp.concatenate(
        [jnp.concatenate([rh, rl], axis=1), jnp.concatenate([rh, jnp.zeros_like(rl)], axis=1)], axis=0
    )
    both = dot(jnp.concatenate([lh, ll], axis=1), weights)
    return both[:, :width] + both[:, width:]


def gram(parts):
    high, low = parts
    rows = jnp.concatenate(
        [jnp.concatenate([high, high], axis=1), jnp.concatenate([low, jnp.zeros_like(low)], axis=1)], axis=0
    )
    both = lax.dot_general(
        jnp.concatenate([high, low], axis=1), rows, (((1,), (1,)), ((), ())), preferred_element_type=f32
    )
    return both[:, : high.shape[0]] + both[:, high.shape[0] :]


def orthogonalize(gradients):
    current = [
        g * lax.rsqrt(jnp.sum(jnp.sum(g * g, axis=1, keepdims=True), axis=0, keepdims=True) + EPSILON)
        for g in gradients
    ]
    for _ in range(NS_STEPS):
        parts = [two_parts(x) for x in current]
        square = [gram(p) for p in parts]
        halves = [two_parts(s) for s in square]
        polynom = [MUON_B * s + MUON_C * dot_parts(h, h) for s, h in zip(square, halves)]
        current = [
            MUON_A * x + dot_parts(two_parts(q), p) for x, q, p in zip(current, polynom, parts)
        ]
    return current


def moved_on(weights, step, direction, axis):
    moved = weights + step * direction
    before = jnp.sqrt(jnp.sum(weights * weights, axis=axis, keepdims=True) + EPSILON)
    after = jnp.sqrt(jnp.sum(moved * moved, axis=axis, keepdims=True) + EPSILON)
    return moved * (before / after)


def encode(weights, inverse_unit):
    codes = jnp.clip(jnp.round(weights * inverse_unit), -CODES, CODES)
    return codes.astype(jnp.int32).astype(jnp.int16)


def decode(codes, unit):
    return codes.astype(jnp.int32).astype(f32) * unit


def setup_body(slack, init_ref, code_ref, unit_ref, inverse_ref):
    for index in range(init_ref.shape[0]):
        weights = init_ref[index]
        down = index % 3 == 2
        if down:
            weights = weights.T
        total = jnp.sum(weights * weights, axis=1 if down else 0, keepdims=True) + slack
        unit = jnp.broadcast_to(jnp.sqrt(total) * (1.001 / CODES), weights.shape)
        inverse = 1.0 / unit
        unit_ref[index] = unit
        inverse_ref[index] = inverse
        code_ref[index] = encode(weights, inverse)


def setup(fast_init, groups):
    flat = fast_init.reshape((-1,) + fast_init.shape[-2:])
    return pl.pallas_call(
        functools.partial(setup_body, (groups + 2) * EPSILON),
        out_shape=(
            jax.ShapeDtypeStruct(flat.shape, jnp.int16),
            jax.ShapeDtypeStruct(flat.shape, f32),
            jax.ShapeDtypeStruct(flat.shape, f32),
        ),
        in_specs=[on_chip()],
        out_specs=(on_chip(),) * 3,
        compiler_params=params(20),
        name="setup",
    )(flat)


def pack_body(x_ref, o_ref):
    rows, width = x_ref.shape
    heads = width // LANES
    total = jnp.zeros((rows, LANES), f32)
    for head in range(heads):
        piece = x_ref[:, head * LANES : (head + 1) * LANES]
        o_ref[head, :rows, :] = piece
        wide = piece.astype(f32)
        total = total + wide * wide
    lines = [
        jnp.sum(total[r * LANES : (r + 1) * LANES].T, axis=0, keepdims=True) for r in range(rows // LANES)
    ]
    inverse = lax.rsqrt(jnp.concatenate(lines, axis=0) / width + EPSILON)
    high = inverse.astype(bf16).astype(f32)
    middle = (inverse - high).astype(bf16).astype(f32)
    low = inverse - high - middle
    tail = jnp.concatenate([high, middle, low, jnp.zeros_like(low)], axis=0).astype(bf16)
    for head in range(heads):
        o_ref[head, rows:, :] = tail


def pack(x):
    rows, width = x.shape
    tail = 4 * (rows // LANES)
    return pl.pallas_call(
        pack_body,
        out_shape=jax.ShapeDtypeStruct((width // LANES, rows + tail, LANES), bf16),
        compiler_params=params(20),
        name="pack",
    )(x)


def column_of(lines):
    count = lines.shape[0]
    return jnp.concatenate([lines] * (8 // count), axis=0).T


def prep_body(inverse_inside, rows, *refs):
    if inverse_inside:
        x_ref, rate_ref, gain_ref, early_ref, late_ref, inverse_out = refs
    else:
        x_ref, inverse_ref, rate_ref, gain_ref, early_ref, late_ref = refs
    lines = rows // LANES
    key, value = gain_ref[0:1, :] * gain_ref[2:3, :], gain_ref[0:1, :] * gain_ref[3:4, :]

    def fill(o_ref):
        for block in range(x_ref.shape[0]):
            if inverse_inside:
                tail = x_ref[block, rows:, :].astype(f32)
                inverse = tail[:lines] + tail[lines : 2 * lines] + tail[2 * lines : 3 * lines]
                inverse_out[block] = inverse
            else:
                inverse = inverse_ref[block]
            inverse = column_of(inverse)
            rate = column_of(rate_ref[block])
            for r in range(lines):
                at = block * rows + r * LANES
                wide = x_ref[block, r * LANES : (r + 1) * LANES, :].astype(f32)
                normed = wide * inverse[:, r : r + 1]
                o_ref[0, at : at + LANES, :] = (normed * key).astype(bf16)
                values = (normed * value).astype(bf16)
                o_ref[1, at : at + LANES, :] = (rate[:, r : r + 1] * values.astype(f32)).astype(bf16)

    half = pl.num_programs(0) // 2

    @pl.when(pl.program_id(0) < half)
    def _():
        fill(early_ref)

    @pl.when(pl.program_id(0) >= half)
    def _():
        fill(late_ref)


def prep(x, inverse, rates, gains, rows):
    blocks, height = x.shape[:2]
    lines = rows // LANES
    step = 8
    half = blocks // step // 2
    pair = jax.ShapeDtypeStruct((2, blocks * rows // 2, LANES), bf16)
    line_spec = pl.BlockSpec((step, lines, LANES), lambda i: (i, 0, 0))
    inside = inverse is None
    shapes = [pair, pair]
    out_specs = [
        pl.BlockSpec((2, step * rows, LANES), lambda i: (0, jnp.minimum(i, half - 1), 0)),
        pl.BlockSpec((2, step * rows, LANES), lambda i: (0, jnp.maximum(i - half, 0), 0)),
    ]
    operands = [x, rates, gains] if inside else [x, inverse, rates, gains]
    in_specs = [pl.BlockSpec((step, height, LANES), lambda i: (i, 0, 0))]
    in_specs += [line_spec] * (len(operands) - 2) + [pl.BlockSpec(gains.shape, lambda i: (0, 0))]
    if inside:
        shapes.append(jax.ShapeDtypeStruct((blocks, lines, LANES), f32))
        out_specs.append(line_spec)
    return pl.pallas_call(
        functools.partial(prep_body, inside, rows),
        out_shape=tuple(shapes),
        grid=(blocks // step,),
        in_specs=in_specs,
        out_specs=tuple(out_specs),
        compiler_params=params(40),
        name="prep",
    )(*operands)


def tick_body(chunk, flag_ref, step_ref, w_ref, unit_ref, inverse_ref, early_ref, late_far, o_ref, kept_ref, late_ref, late_sem):
    updates = flag_ref[0] != 0
    late_in = pltpu.make_async_copy(late_far, late_ref, late_sem)

    @pl.when(updates)
    def _():
        late_in.start()


    @pl.when(jnp.logical_not(updates))
    def _():
        o_ref[...] = w_ref[...]
        kept_ref[...] = w_ref[...]

    @pl.when(updates)
    def _():
        weights = [decode(w_ref[j], unit_ref[j]) for j in range(3)]
        gate_up = jnp.concatenate(
            [0.5 * weights[0].astype(bf16).astype(f32), 0.5 * weights[1].astype(bf16).astype(f32)], axis=1
        ).astype(bf16)
        down = weights[2].astype(bf16)
        over_tokens = functools.partial(
            lax.dot_general, dimension_numbers=(((0,), (0,)), ((), ())), preferred_element_type=f32
        )

        def part(d_ref, at):
            keys = d_ref[0, at : at + chunk, :]
            targets = d_ref[1, at : at + chunk, :]
            both = dot(keys, gate_up)
            back = dot(targets, down)
            half, half_up = both[:, :LANES], both[:, LANES:]
            bent = jnp.tanh(half)
            slope = half * bent
            act = half + slope
            hidden = (act * half_up).astype(bf16)
            back_up = (back * act).astype(bf16)
            rise = (1.0 + bent) * (1.0 + (half - slope))
            back_gate = (back * half_up * rise).astype(bf16)
            return (
                over_tokens(keys, jnp.concatenate([back_gate, back_up], axis=1)),
                over_tokens(targets, hidden),
            )

        first, second = part(early_ref, 0)
        for d_ref, begin in ((early_ref, chunk), (late_ref, 0)):
            if d_ref is late_ref:
                late_in.wait()
            for at in range(begin, d_ref.shape[1], chunk):
                more_first, more_second = part(d_ref, at)
                first = first + more_first
                second = second + more_second
        direction = orthogonalize([first[:, :LANES], first[:, LANES:], 2.0 * second])
        for j in range(3):
            fresh = moved_on(weights[j], step_ref[0], direction[j], 1 if j == 2 else 0)
            o_ref[j] = encode(fresh, inverse_ref[j])
            kept_ref[j] = w_ref[j]


def tick(flag, step, codes, unit, inverse_unit, early, late):
    far = pl.BlockSpec(memory_space=pltpu.HBM)
    scalar = pl.BlockSpec(memory_space=pltpu.SMEM)
    shape = jax.ShapeDtypeStruct(codes.shape, jnp.int16)
    return pl.pallas_call(
        functools.partial(tick_body, min(2048, early.shape[1])),
        out_shape=(shape, shape),
        in_specs=[scalar, scalar, on_chip(), on_chip(), on_chip(), on_chip(), far],
        out_specs=(on_chip(), on_chip()),
        scratch_shapes=[
            pltpu.VMEM(late.shape, bf16),
            pltpu.SemaphoreType.DMA,
        ],
        compiler_params=params(24),
        name="tick",
    )(flag, step, codes, unit, inverse_unit, early, late)


def mix_body(rows, x_ref, inverse_ref, gain_ref, w_ref, unit_ref, _, o_ref, *part_ref):
    weights = [decode(w_ref[j], unit_ref[j]).astype(bf16) for j in range(3)]
    gate_up = jnp.concatenate(weights[:2], axis=1)
    down = weights[2].T
    query, scale = gain_ref[0:1, :] * gain_ref[1:2, :], gain_ref[4:5, :]
    lines = rows // LANES
    blocks = x_ref.shape[0]
    pieces = []
    for block in range(blocks):
        inverse = column_of(inverse_ref[block])
        for r in range(lines):
            wide = x_ref[block, r * LANES : (r + 1) * LANES, :].astype(f32)
            pieces.append((wide * inverse[:, r : r + 1] * query).astype(bf16))
    both = dot(jnp.concatenate(pieces, axis=0), gate_up)
    gate, up = both[:, :LANES], both[:, LANES:]
    hidden = (gate * (0.5 * jnp.tanh(0.5 * gate) + 0.5) * up).astype(bf16)
    output = dot(hidden, down)
    ones = jnp.ones((2 * LANES, LANES), bf16)
    own = lax.broadcasted_iota(jnp.int32, (LANES, LANES), 0) == lax.broadcasted_iota(jnp.int32, (LANES, LANES), 1)
    for block in range(blocks):
        mixed = (x_ref[block].astype(f32) + scale * output[block * rows : (block + 1) * rows]).astype(bf16)
        o_ref[block] = mixed
        if part_ref:
            square = mixed.astype(f32)
            total = dot(jnp.concatenate(two_parts(square * square), axis=1), ones)
            part_ref[0][block] = jnp.concatenate(
                [
                    jnp.sum(jnp.where(own, total[r * LANES : (r + 1) * LANES], 0.0), axis=0, keepdims=True)
                    for r in range(lines)
                ],
                axis=0,
            )


def mix(x, inverse, gains, codes, unit, after, rows, sums):
    blocks = x.shape[0]
    step = 8
    lines = rows // LANES
    whole = lambda i: (0, 0)
    cube = lambda i: (0, 0, 0)
    moving = lambda i: (i, 0, 0)
    shapes = [(pltpu.HBM if sums else jax.ShapeDtypeStruct)((blocks, rows, LANES), bf16)]
    out_specs = [pl.BlockSpec((step, rows, LANES), moving)]
    if sums:
        shapes.append(jax.ShapeDtypeStruct((blocks, lines, LANES), f32))
        out_specs.append(pl.BlockSpec((step, lines, LANES), moving))
    return pl.pallas_call(
        functools.partial(mix_body, rows),
        out_shape=tuple(shapes),
        grid=(blocks // step,),
        in_specs=[
            pl.BlockSpec((step, rows, LANES), moving),
            pl.BlockSpec((step, lines, LANES), moving),
            pl.BlockSpec(gains.shape, whole),
            pl.BlockSpec(codes.shape, cube),
            pl.BlockSpec(unit.shape, cube),
            pl.BlockSpec(memory_space=pl.ANY),
        ],
        out_specs=tuple(out_specs),
        compiler_params=params(40),
        name="mix",
    )(x, inverse, gains, codes, unit, after)


def unpack_body(x_ref, o_ref):
    for head in range(x_ref.shape[0]):
        o_ref[:, head * LANES : (head + 1) * LANES] = x_ref[head]


def unpack(x):
    heads, rows, lanes = x.shape
    step = min(rows, 256)
    return pl.pallas_call(
        unpack_body,
        out_shape=jax.ShapeDtypeStruct((rows, heads * lanes), x.dtype),
        grid=(rows // step,),
        in_specs=[pl.BlockSpec((heads, step, lanes), lambda i: (0, i, 0))],
        out_specs=pl.BlockSpec((step, heads * lanes), lambda i: (i, 0)),
        compiler_params=params(20),
        name="unpack",
    )(x)


def passed_on(value, index, groups):
    def hop(target):
        return lambda sent: lax.ppermute(sent, "group", [(target - 1, target)])

    return lax.switch(index, [lambda sent: sent] + [hop(target) for target in range(1, groups)], value)


def held_back(state, me, groups):
    row = 4
    targets = list(range(row - 1, groups - row - 1, row))
    if not targets:
        return jnp.zeros((8, LANES), f32)
    source = targets[-1] + row

    def release(state):
        seed = state[0, :8, :].astype(f32)
        return sum(lax.ppermute(seed, "group", [(source, target)]) for target in targets)

    joins = functools.reduce(jnp.logical_or, [me == group for group in targets + [source]])
    return lax.cond(joins, release, lambda state: jnp.zeros((8, LANES), f32), state)


def summed_over(value, axis):
    size = lax.axis_size(axis)
    bit = 1
    while bit < size:
        value = value + lax.ppermute(value, axis, [(i, i ^ bit) for i in range(size)])
        bit *= 2
    return value


def body(tokens, learning_rates, channel_gains, fast_init, step_size, update_table):
    groups = lax.axis_size("group")
    ranks = lax.axis_size("tok")
    me = lax.axis_index("group")
    rows, width = tokens.shape
    layers = fast_init.shape[0]
    lines = rows // LANES

    codes, unit, inverse_unit = setup(fast_init, groups)
    rates = learning_rates.reshape(layers, ranks, lines, LANES)
    stream = lax.all_to_all(pack(tokens), "tok", split_axis=0, concat_axis=0, tiled=True)
    inverse = None

    for layer in range(layers):
        chosen = slice(3 * layer, 3 * layer + 3)
        stream = pltpu.with_memory_space_constraint(stream, pltpu.HBM)
        prepared = prep(stream, inverse, rates[layer], channel_gains[layer], rows)
        if inverse is None:
            inverse = prepared[2]
        early = pltpu.with_memory_space_constraint(prepared[0], pltpu.VMEM)
        late = prepared[1]
        flag = lax.dynamic_slice(update_table[layer], (me,), (1,))
        flag = jnp.where(me < groups - 1, flag, 0)
        step = step_size[layer]
        layer_unit, layer_inverse = unit[chosen], inverse_unit[chosen]

        def one(index, held):
            arrived = passed_on(held[0], index, groups)
            return lax.cond(
                index == me,
                lambda now, _: tick(flag, step, now, layer_unit, layer_inverse, early, late),
                lambda now, before: (now, before),
                arrived,
                held[1],
            )

        first = codes[chosen]
        _, entering = lax.fori_loop(me, jnp.minimum(me + 2, groups), one, (first, first))
        last = layer + 1 == layers
        after = held_back(entering, me, groups) if last else jnp.zeros((8, LANES), f32)
        outcome = mix(stream, inverse, channel_gains[layer], entering, layer_unit, after, rows, not last)
        stream = outcome[0]
        if not last:
            inverse = lax.rsqrt(summed_over(outcome[1], "tok") / width + EPSILON)
    return unpack(lax.all_to_all(stream, "tok", split_axis=0, concat_axis=0, tiled=True))


def solution(mesh):
    in_specs = (
        P(("group", "tok"), None),
        P(None, "group"),
        P(None, None, "tok"),
        P(None, None, "tok", None, None),
        P(None, "tok"),
        P(),
    )
    out_specs = P(("group", "tok"), None)
    return jax.shard_map(body, mesh=mesh, in_specs=in_specs, out_specs=out_specs, check_vma=False)
```
